256 devices in a mesh: row: 16 (over z, core), col: 16 (over x, y).
Axes of the slice: x: 4, y: 4, z: 8, core: 2. Of those that a mesh axis runs over, the one named last changes fastest.
Arguments:
- token_ids: int32 [32, 256], P('row'), may hold values from 0 to 16383
- passage_lengths: int32 [32], P('row'), may hold values from 64 to 256, as said below
- embedding: bfloat16 [16384, 4096], P(None, 'col'), may hold values from -8 to 8
- attn_gain: bfloat16 [4096], P('col'), may hold values from 0.25 to 1.75
- final_gain: bfloat16 [4096], P('col'), may hold values from 0.25 to 1.75
- query_weight: bfloat16 [4096, 4096], P('row', 'col'), may hold values from -0.5 to 0.5
- key_weight: bfloat16 [4096, 4096], P('row', 'col'), may hold values from -0.5 to 0.5
- value_weight: bfloat16 [4096, 4096], P('row', 'col'), may hold values from -0.09375 to 0.09375
- out_weight: bfloat16 [4096, 4096], P('row', 'col'), may hold values from -0.09375 to 0.09375
- crosskey_weight: bfloat16 [4096, 4096], P('row', 'col'), may hold values from -0.09375 to 0.09375
- crossvalue_weight: bfloat16 [4096, 4096], P('row', 'col'), may hold values from -0.09375 to 0.09375
Outputs:
- hidden_out: bfloat16 [8192, 4096], P('row', 'col')
- cross_keys: bfloat16 [8192, 16, 256], P('row', 'col')
- cross_values: bfloat16 [8192, 16, 256], P('row', 'col')
The draws below stay inside these ranges and needn't reach their ends.
Inputs may be any that keep to these rules, and one draw needn't show every extreme that they name: `passage_lengths`: some passage of every draw has all 256 slots valid.
All inputs are finite; a program needn't handle non-finite values.
Results may differ from the reference program's by a relative error of at most 0.0082.
Values may be sent and summed in bfloat16 or wider, within the bound.
No kernel may reach another device: no remote copies, remote signals or barrier semaphores. Data moves between devices by JAX's collectives and lax.ppermute only.
A program may use at most 64 MiB of HBM per device.

```python
import math
import jax
import jax.numpy as jnp
import numpy as np
from jax import lax

D = 4096
HEADS = 16
HD = 256
VOCAB = 16384
PLEN = 256
PASSAGES = 32
TOKENS = 8192


def draw_passage_lengths(key, part):
    first_key = jax.random.fold_in(key, 11)
    second_key = jax.random.fold_in(key, 12)
    drawn = jax.random.randint(first_key, (PASSAGES,), PLEN // 4, PLEN + 1)
    chosen = jax.random.randint(second_key, (), 0, PASSAGES)
    return jnp.where(jnp.arange(PASSAGES) == chosen, PLEN, drawn).astype(jnp.int32)


def draw_embedding(key, part):
    base_key = jax.random.fold_in(key, 21)
    row_key = jax.random.fold_in(key, 22)
    col_key = jax.random.fold_in(key, 23)
    row_scale = jnp.exp(jax.random.uniform(row_key, (VOCAB, 1), jnp.float32, math.log(0.15), math.log(1.5)))
    rising = jnp.exp(math.log(3.0) * (jnp.arange(D, dtype=jnp.float32) / D - 0.5))
    col_scale = rising[None, :] * jnp.exp(jax.random.uniform(col_key, (1, D), jnp.float32, math.log(0.6), math.log(1.8)))
    values = jax.random.normal(base_key, (VOCAB, D), jnp.float32) * row_scale * col_scale
    return jnp.clip(values, -8.0, 8.0).astype(jnp.bfloat16)


def shared_projection(key, salt):
    own = jax.random.normal(jax.random.fold_in(key, salt), (D, D), jnp.float32) / math.sqrt(D)
    values = own
    return jnp.clip(values, -0.5, 0.5).astype(jnp.bfloat16)


def draw_query_weight(key, part):
    return shared_projection(key, 31)


def draw_key_weight(key, part):
    return shared_projection(key, 32)


def set_ends(entries, own_key, smallest, largest):
    longest = entries.shape.index(max(entries.shape))
    spots = []
    for shift in (0, 1):
        where = [jax.random.randint(jax.random.fold_in(own_key, axis), (), 0, length) for axis, length in enumerate(entries.shape)]
        where[longest] = (where[longest] + shift) % entries.shape[longest]
        spots.append(tuple(where))
    return entries.at[spots[0]].set(smallest).at[spots[1]].set(largest)


def shard_levels(stream_key, shape, shards, least, top_value):
    factor_of = 1.0
    for position, parts in shards:
        steps = jax.random.uniform(jax.random.fold_in(jax.random.fold_in(stream_key, 6), position), (parts,), jnp.float32, least / len(shards), top_value / len(shards))
        factor_of = factor_of * jnp.repeat(jnp.exp(steps), shape[position] // parts).reshape((-1,) + (1,) * (len(shape) - 1 - position))
    return factor_of


def cumulative_ranks(amount, slope):
    loads = [(1 << 20) // math.isqrt(standing ** slope) + 1 for standing in range(1, amount + 1)]
    scale = 1 + sum(loads) // (1 << 30)
    return np.cumsum(np.array([max(1, weight // scale) for weight in loads]))


def ranked(stream_key, dims, amount, lean):
    listing = cumulative_ranks(amount, lean)
    lot = jax.random.randint(jax.random.fold_in(stream_key, 1), dims, 0, int(listing[amount - 1]))
    grade = jnp.searchsorted(jnp.asarray(listing, jnp.int32), lot, side="right")
    return jax.random.permutation(jax.random.fold_in(stream_key, 2), amount)[grade].astype(jnp.int32)


def gaussian(key, shape, scale, bound, shards=(), kind=jnp.bfloat16):
    entries = scale * jax.random.normal(key, shape, jnp.float32)
    if shards:
        entries = entries * shard_levels(key, shape, shards, -0.22, 0.18)
    return jnp.clip(entries, -bound, bound).astype(kind)


def setup_inputs(seed: int = 0) -> dict:
    arg_keys = jax.random.split(jax.random.key(seed), 12)
    return {
        "token_ids": set_ends(ranked(arg_keys[0], (PASSAGES, PLEN), VOCAB, 2), jax.random.fold_in(arg_keys[0], 3), 0, VOCAB - 1).astype(jnp.int32),
        "passage_lengths": draw_passage_lengths(jax.random.fold_in(arg_keys[11], 71), 0),
        "embedding": draw_embedding(jax.random.fold_in(arg_keys[11], 71), 0),
        "attn_gain": jnp.clip(1.0 + 0.15 * jax.random.normal(arg_keys[3], (D,), jnp.float32), 0.25, 1.75).astype(jnp.bfloat16),
        "final_gain": jnp.clip(1.0 + 0.15 * jax.random.normal(arg_keys[4], (D,), jnp.float32), 0.25, 1.75).astype(jnp.bfloat16),
        "query_weight": draw_query_weight(jax.random.fold_in(arg_keys[11], 71), 0),
        "key_weight": draw_key_weight(jax.random.fold_in(arg_keys[11], 71), 0),
        "value_weight": gaussian(arg_keys[7], (D, D), D ** -0.5, 0.09375, ((0, 16), (1, 16))),
        "out_weight": gaussian(arg_keys[8], (D, D), D ** -0.5, 0.09375, ((0, 16), (1, 16))),
        "crosskey_weight": gaussian(arg_keys[9], (D, D), D ** -0.5, 0.09375, ((0, 16), (1, 16))),
        "crossvalue_weight": gaussian(arg_keys[10], (D, D), D ** -0.5, 0.09375, ((0, 16), (1, 16))),
    }


epsilon = 1e-06
masked_score = -1000000000.0

def rms_norm(row_block, gain_row):
    widened = row_block.astype(jnp.float32)
    mean_square = lax.optimization_barrier(jnp.mean(widened * widened, axis=1, keepdims=True))
    return (widened * lax.rsqrt(mean_square + epsilon) * gain_row.astype(jnp.float32)).astype(jnp.bfloat16)

def project(activ, weight):
    return jnp.dot(activ, weight, preferred_element_type=jnp.float32)

def reference(token_ids, passage_lengths, embedding, attn_gain, final_gain, query_weight, key_weight, value_weight, out_weight, crosskey_weight, crossvalue_weight):
    embedded = jnp.take(embedding, token_ids.reshape(-1), axis=0)
    normed = rms_norm(embedded, attn_gain)
    query_rows = project(normed, query_weight).astype(jnp.bfloat16)
    key_rows = project(normed, key_weight).astype(jnp.bfloat16)
    value_rows = project(normed, value_weight).astype(jnp.bfloat16)
    query_four = query_rows.astype(jnp.float32).reshape(PASSAGES, PLEN, HEADS, HD)
    key_four = key_rows.astype(jnp.float32).reshape(PASSAGES, PLEN, HEADS, HD)
    value_four = value_rows.astype(jnp.float32).reshape(PASSAGES, PLEN, HEADS, HD)
    scores = jnp.einsum('pihd,pjhd->phij', query_four, key_four) * HD ** (-0.5)
    valid = jnp.arange(PLEN, dtype=jnp.int32)[None, :] < passage_lengths[:, None]
    scores = jnp.where(valid[:, None, None, :], scores, masked_score)
    highest = lax.optimization_barrier(jnp.max(scores, axis=-1, keepdims=True))
    expon = jnp.exp(scores - highest)
    probs = (expon / lax.optimization_barrier(jnp.sum(expon, axis=-1, keepdims=True))).astype(jnp.bfloat16)
    attended = jnp.einsum('phij,pjhd->pihd', probs.astype(jnp.float32), value_four)
    attended = attended.astype(jnp.bfloat16).reshape(TOKENS, D)
    hidden_out = (embedded.astype(jnp.float32) + project(attended, out_weight)).astype(jnp.bfloat16)
    final_normed = rms_norm(hidden_out, final_gain)
    cross_keys = project(final_normed, crosskey_weight).astype(jnp.bfloat16).reshape(TOKENS, HEADS, HD)
    cross_values = project(final_normed, crossvalue_weight).astype(jnp.bfloat16).reshape(TOKENS, HEADS, HD)
    return (hidden_out, cross_keys, cross_values)
```

```python
import jax
import jax.numpy as jnp
from jax import lax
from jax.experimental import pallas as pl
from jax.experimental.pallas import tpu as pltpu
from jax.sharding import PartitionSpec as P

D = 4096
HD = 256
PLEN = 256
SIDE = 4
BLOCKS = SIDE * SIDE
GAIN_ROWS = 16

epsilon = 1e-06
masked_score = -1000000000.0


SHIFTS = (1, 3, 2)
OFFSETS = (0, 3, 1, 2)
ANY = pl.BlockSpec(memory_space=pl.ANY)
SMEM = pl.BlockSpec(memory_space=pltpu.SMEM)
VMEM = pl.BlockSpec(memory_space=pltpu.VMEM)


def along_x(shift):
    return [
        (x * SIDE + y, (x + shift) % SIDE * SIDE + y)
        for x in range(SIDE)
        for y in range(SIDE)
    ]


def along_y(shift):
    return [
        (x * SIDE + y, x * SIDE + (y + shift) % SIDE)
        for x in range(SIDE)
        for y in range(SIDE)
    ]


def spread(chunk, axis_pairs):
    return [chunk] + [lax.ppermute(chunk, "col", axis_pairs(s)) for s in SHIFTS]


def gather_plane(chunk_a, chunk_b):
    first_a = spread(chunk_a, along_x)
    first_b = spread(chunk_b, along_y)
    stack_a = jnp.stack(first_a)
    stack_b = jnp.stack(first_b)
    return spread(stack_a, along_y) + spread(stack_b, along_x)


def block_of(col, a, b):
    x = lax.rem(lax.div(col, SIDE) + OFFSETS[a], SIDE)
    y = lax.rem(lax.rem(col, SIDE) + OFFSETS[b], SIDE)
    return x * SIDE + y


def row_copies(col, parts_a, parts_b, rows, sem, gains=None, gain_sem=None):
    copies = []
    for a in range(SIDE):
        for b in range(SIDE):
            place = pl.ds(pl.multiple_of(block_of(col, a, b) * HD, HD), HD)
            spot = a * SIDE + b
            copies.append(
                pltpu.make_async_copy(
                    parts_a[b].at[a, pl.ds(0, PLEN)],
                    rows.at[pl.ds(0, PLEN), place],
                    sem.at[0, spot],
                )
            )
            copies.append(
                pltpu.make_async_copy(
                    parts_b[a].at[b],
                    rows.at[pl.ds(PLEN, PLEN), place],
                    sem.at[1, spot],
                )
            )
            if gains is not None:
                copies.append(
                    pltpu.make_async_copy(
                        parts_a[b].at[a, pl.ds(PLEN, GAIN_ROWS)],
                        gains.at[:, place],
                        gain_sem.at[spot],
                    )
                )
    return copies


def scale_rows(rows, gain, inverse):
    step, width = 32, 512

    @pl.loop(0, rows.shape[0] // step)
    def _(tile):
        here = pl.ds(pl.multiple_of(tile * step, step), step)
        total = jnp.zeros((step, 128), jnp.float32)
        for part in range(D // width):
            cols = pl.ds(part * width, width)
            wide = rows[here, cols].astype(jnp.float32)
            square = wide * wide
            for lane in range(width // 128):
                total += square[:, lane * 128 : (lane + 1) * 128]
            rows[here, cols] = (wide * gain[:, cols]).astype(jnp.bfloat16)
        mean = jnp.sum(total, axis=1, keepdims=True) / D
        inverse[here, :] = lax.rsqrt(mean + epsilon)


def attend_kernel(*refs):
    col_ref, len_ref = refs[:2]
    parts_a, parts_b = refs[2:6], refs[6:10]
    weight, out_a, out_b, final_ref = refs[10:14]
    rows, held, heads, gains, gain_row, inverse, sem, gain_sem, weight_sem = refs[14:]
    copies = row_copies(col_ref[0], parts_a, parts_b, rows, sem, gains, gain_sem)
    for copy in copies:
        copy.start()
    load = pltpu.make_async_copy(weight, held, weight_sem)
    load.start()
    for copy in copies:
        copy.wait()
    gain_row[...] = gains[0:1, :].astype(jnp.float32)
    final_ref[...] = gains[1:2, :].astype(jnp.float32)
    scale_rows(rows, gain_row, inverse)
    load.wait()

    @pl.loop(0, 2)
    def _(p):
        here = pl.ds(pl.multiple_of(p * PLEN, PLEN), PLEN)
        total = jnp.dot(rows[here, :], held[...], preferred_element_type=jnp.float32)
        heads[here, :] = (total * inverse[here, :]).astype(jnp.bfloat16)

    for p, out in enumerate((out_a, out_b)):
        here = pl.ds(p * PLEN, PLEN)
        query, key, value = (heads[here, i * HD : (i + 1) * HD] for i in range(3))
        scores = lax.dot_general(
            query, key, (((1,), (1,)), ((), ())), preferred_element_type=jnp.float32
        ) * HD ** (-0.5)
        slot = lax.broadcasted_iota(jnp.int32, (PLEN, PLEN), 1)
        scores = jnp.where(slot < len_ref[p], scores, masked_score)
        expon = jnp.exp(scores - jnp.max(scores, axis=-1, keepdims=True))
        probs = (expon / jnp.sum(expon, axis=-1, keepdims=True)).astype(jnp.bfloat16)
        out[...] = jnp.dot(probs, value, preferred_element_type=jnp.float32).astype(jnp.bfloat16)


def residual_kernel(*refs):
    col_ref = refs[0]
    parts_a, parts_b = refs[1:5], refs[5:9]
    weight, embedded, out, out_a, out_b = refs[9:14]
    rows, held, sem, weight_sem = refs[14:]
    load = pltpu.make_async_copy(weight.at[:, pl.ds(0, HD)], held, weight_sem)
    load.start()
    copies = row_copies(col_ref[0], parts_a, parts_b, rows, sem)
    for copy in copies:
        copy.start()
    load.wait()
    for copy in copies:
        copy.wait()

    @pl.loop(0, 2)
    def _(p):
        here = pl.ds(pl.multiple_of(p * PLEN, PLEN), PLEN)
        total = jnp.dot(rows[here, :], held[...], preferred_element_type=jnp.float32)
        out[here, :] = (embedded[here, :].astype(jnp.float32) + total).astype(jnp.bfloat16)

    out_a[...] = out[:PLEN, :]
    out_b[...] = out[PLEN:, :]


def cross_kernel(*refs):
    col_ref = refs[0]
    parts_a, parts_b = refs[1:5], refs[5:9]
    weight, gain_row, keys, values = refs[9:13]
    rows, held, inverse, sem, weight_sem = refs[13:]
    copies = row_copies(col_ref[0], parts_a, parts_b, rows, sem)
    for copy in copies:
        copy.start()
    load = pltpu.make_async_copy(weight.at[:, pl.ds(HD, 2 * HD)], held, weight_sem)
    load.start()
    for copy in copies:
        copy.wait()
    scale_rows(rows, gain_row, inverse)
    load.wait()

    @pl.loop(0, 2)
    def _(p):
        here = pl.ds(pl.multiple_of(p * PLEN, PLEN), PLEN)
        head = jnp.dot(rows[here, :], held[...], preferred_element_type=jnp.float32)
        head = (head * inverse[here, :]).astype(jnp.bfloat16)
        keys[here, :] = head[:, :HD]
        values[here, :] = head[:, HD:]


def bf16(*shape):
    return jax.ShapeDtypeStruct(shape, jnp.bfloat16)


def params():
    return pltpu.CompilerParams(vmem_limit_bytes=40 << 20)


def shards(
    token_ids,
    passage_lengths,
    embedding,
    attn_gain,
    final_gain,
    query_weight,
    key_weight,
    value_weight,
    out_weight,
    crosskey_weight,
    crossvalue_weight,
):
    early = lax.all_gather(
        jnp.concatenate([query_weight, key_weight, value_weight], axis=1), "row", axis=0, tiled=True
    )
    late = lax.all_gather(
        jnp.concatenate([out_weight, crosskey_weight, crossvalue_weight], axis=1),
        "row",
        axis=0,
        tiled=True,
    )
    col = lax.axis_index("col").astype(jnp.int32).reshape(1)
    embedded = embedding.at[token_ids.reshape(-1)].get(mode="promise_in_bounds")
    gains = jnp.concatenate(
        [
            attn_gain[None, :],
            final_gain[None, :],
            jnp.zeros((GAIN_ROWS - 2, HD), jnp.bfloat16),
        ],
        axis=0,
    )
    chunk_a = jnp.concatenate([embedded[:PLEN], gains], axis=0)
    chunk_b = embedded[PLEN:]
    tokens = 2 * PLEN
    copy_sem = pltpu.SemaphoreType.DMA((2, BLOCKS))
    attended_a, attended_b, final_row = pl.pallas_call(
        attend_kernel,
        out_shape=(bf16(PLEN, HD), bf16(PLEN, HD), jax.ShapeDtypeStruct((1, D), jnp.float32)),
        in_specs=[SMEM, SMEM] + [ANY] * 9,
        out_specs=(VMEM, VMEM, VMEM),
        scratch_shapes=[
            pltpu.VMEM((tokens, D), jnp.bfloat16),
            pltpu.VMEM((D, 3 * HD), jnp.bfloat16),
            pltpu.VMEM((tokens, 3 * HD), jnp.bfloat16),
            pltpu.VMEM((GAIN_ROWS, D), jnp.bfloat16),
            pltpu.VMEM((1, D), jnp.float32),
            pltpu.VMEM((tokens, 1), jnp.float32),
            copy_sem,
            pltpu.SemaphoreType.DMA((BLOCKS,)),
            pltpu.SemaphoreType.DMA,
        ],
        compiler_params=params(),
        cost_estimate=pl.CostEstimate(flops=2 * tokens * D * 3 * HD, bytes_accessed=10 << 20, transcendentals=0),
        name="attend",
    )(col, passage_lengths, *gather_plane(chunk_a, chunk_b), early)
    hidden, hidden_a, hidden_b = pl.pallas_call(
        residual_kernel,
        out_shape=(bf16(tokens, HD), bf16(PLEN, HD), bf16(PLEN, HD)),
        in_specs=[SMEM] + [ANY] * 9 + [VMEM],
        out_specs=(VMEM, VMEM, VMEM),
        scratch_shapes=[
            pltpu.VMEM((tokens, D), jnp.bfloat16),
            pltpu.VMEM((D, HD), jnp.bfloat16),
            copy_sem,
            pltpu.SemaphoreType.DMA,
        ],
        compiler_params=params(),
        cost_estimate=pl.CostEstimate(flops=2 * tokens * D * HD, bytes_accessed=6 << 20, transcendentals=0),
        name="residual",
    )(col, *gather_plane(attended_a, attended_b), late, embedded)
    cross_keys, cross_values = pl.pallas_call(
        cross_kernel,
        out_shape=(bf16(tokens, HD), bf16(tokens, HD)),
        in_specs=[SMEM] + [ANY] * 9 + [VMEM],
        out_specs=(VMEM, VMEM),
        scratch_shapes=[
            pltpu.VMEM((tokens, D), jnp.bfloat16),
            pltpu.VMEM((D, 2 * HD), jnp.bfloat16),
            pltpu.VMEM((tokens, 1), jnp.float32),
            copy_sem,
            pltpu.SemaphoreType.DMA,
        ],
        compiler_params=params(),
        cost_estimate=pl.CostEstimate(flops=2 * tokens * D * 2 * HD, bytes_accessed=8 << 20, transcendentals=0),
        name="cross",
    )(col, *gather_plane(hidden_a, hidden_b), late, final_row)
    return (
        hidden,
        cross_keys.reshape(tokens, 1, HD),
        cross_values.reshape(tokens, 1, HD),
    )


def solution(mesh):
    return jax.shard_map(
        shards,
        mesh=mesh,
        in_specs=(
            P("row", None),
            P("row"),
            P(None, "col"),
            P("col"),
            P("col"),
            P("row", "col"),
            P("row", "col"),
            P("row", "col"),
            P("row", "col"),
            P("row", "col"),
            P("row", "col"),
        ),
        out_specs=(P("row", "col"), P("row", "col", None), P("row", "col", None)),
        check_vma=False,
    )
```

```python
import functools

import jax
import jax.numpy as jnp
from jax import lax
from jax.experimental import pallas as pl
from jax.experimental.pallas import tpu as pltpu
from jax.sharding import PartitionSpec as P

D = 4096
HD = 256
PLEN = 256
SIDE = 4
BLOCKS = SIDE * SIDE
GAIN_ROWS = 16

epsilon = 1e-06
masked_score = -1000000000.0


ANY = pl.BlockSpec(memory_space=pl.ANY)
SMEM = pl.BlockSpec(memory_space=pltpu.SMEM)
VMEM = pl.BlockSpec(memory_space=pltpu.VMEM)

DEPTH = 8
SHIFTS = (1, 3, 2)
OFFSETS = (0, 3, 1, 2)


def moves(step):
    def index(z, c, x, y):
        return ((z % DEPTH * 2 + c) * SIDE + x % SIDE) * SIDE + y % SIDE

    return [
        (index(z, c, x, y), index(*step(z, c, x, y)))
        for z in range(DEPTH)
        for c in range(2)
        for x in range(SIDE)
        for y in range(SIDE)
    ]


def send(block, step):
    return lax.ppermute(block, ("row", "col"), moves(step))


def first_leg(block, shift):
    return send(block, lambda z, c, x, y: (z, c, x + shift * (1 - c), y + shift * c))


def second_leg(block, shift):
    return send(block, lambda z, c, x, y: (z, c, x + shift * c, y + shift * (1 - c)))


def along_z(block):
    return send(block, lambda z, c, x, y: (z + 1 - 2 * c, c, x, y))


def swap_cores(block):
    return send(block, lambda z, c, x, y: (z, 1 - c, x, y))


def gather_first(chunk):
    return jnp.stack([chunk] + [first_leg(chunk, s) for s in SHIFTS])


def gather_direct(chunk):
    stack = gather_first(chunk)
    return [stack] + [second_leg(stack, s) for s in SHIFTS]


def gather_halved(chunk):
    stack = gather_first(chunk)
    back, ahead = second_leg(stack, 1), second_leg(stack, 3)
    return [stack, back, ahead, second_leg(back[:2], 1), second_leg(ahead[2:], 3)]


def gather_weight(shard):
    other = swap_cores(shard)
    block = jnp.stack([shard, other])
    parts = [shard, other]
    for hop in range(1, DEPTH // 2 + 1):
        block = along_z(block if hop < DEPTH // 2 else block[0])
        parts += [block, swap_cores(block)]
    return parts


def weight_places(place):
    z, c = place[0], place[1]
    up = 1 - 2 * c

    def row(depth, core):
        return lax.rem(depth + DEPTH, DEPTH) * 2 + core

    places = [(0, None, row(z, c)), (1, None, row(z, 1 - c))]
    for hop in range(1, DEPTH // 2):
        places += [(2 * hop, 0, row(z - hop * up, c)), (2 * hop, 1, row(z - hop * up, 1 - c))]
        places += [(2 * hop + 1, 0, row(z + hop * up, 1 - c)), (2 * hop + 1, 1, row(z + hop * up, c))]
    last = DEPTH // 2
    return places + [(2 * last, None, row(z + last, c)), (2 * last + 1, None, row(z + last, 1 - c))]


def weight_copies(place, parts, held, sem):
    copies = []
    for n, (part, spot, row) in enumerate(weight_places(place)):
        source = parts[part] if spot is None else parts[part].at[spot]
        target = held.at[pl.ds(pl.multiple_of(row * HD, HD), HD)]
        copies.append(pltpu.make_async_copy(source, target, sem.at[n]))
    return copies


def block_of(place, first, second):
    c = place[1]
    x = place[2] + OFFSETS[first] * (1 - c) + OFFSETS[second] * c
    y = place[3] + OFFSETS[first] * c + OFFSETS[second] * (1 - c)
    return lax.rem(x, SIDE) * SIDE + lax.rem(y, SIDE)


def row_copies(place, parts, rows, sem, start=0):
    copies = []
    count = rows.shape[0]
    for first in range(SIDE):
        for second in range(SIDE):
            where = pl.ds(pl.multiple_of(block_of(place, first, second) * HD, HD), HD)
            if second < 3 or len(parts) == 4:
                source = parts[second].at[first]
            else:
                source = parts[3 + first // 2].at[first % 2]
            copies.append(
                pltpu.make_async_copy(
                    source.at[pl.ds(start, count)],
                    rows.at[:, where],
                    sem.at[first * SIDE + second],
                )
            )
    return copies


def read(place_ref):
    row, col = place_ref[0], place_ref[1]
    return [lax.div(row, 2), lax.rem(row, 2), lax.div(col, SIDE), lax.rem(col, SIDE)]


def start_all(copies):
    for copy in copies:
        copy.start()


def wait_all(copies):
    for copy in copies:
        copy.wait()


def scale_rows(rows, gain, inverse):
    step, width = 32, 512

    @pl.loop(0, rows.shape[0] // step)
    def _(tile):
        here = pl.ds(pl.multiple_of(tile * step, step), step)
        total = jnp.zeros((step, 128), jnp.float32)
        for part in range(D // width):
            cols = pl.ds(part * width, width)
            wide = rows[here, cols].astype(jnp.float32)
            square = wide * wide
            for lane in range(width // 128):
                total += square[:, lane * 128 : (lane + 1) * 128]
            rows[here, cols] = (wide * gain[:, cols]).astype(jnp.bfloat16)
        mean = jnp.sum(total, axis=1, keepdims=True) / D
        inverse[here, :] = lax.rsqrt(mean + epsilon)


def prepare_kernel(*refs):
    place = read(refs[0])
    parts = refs[1:5]
    rows, inverse, final_ref, gains, gain_row, sem, gain_sem = refs[5:]
    copies = row_copies(place, parts, gains, gain_sem, rows.shape[0]) + row_copies(place, parts, rows, sem)
    start_all(copies)
    wait_all(copies)
    gain_row[...] = gains[0:1, :].astype(jnp.float32)
    final_ref[...] = gains[1:2, :].astype(jnp.float32)
    scale_rows(rows, gain_row, inverse)


def attend_kernel(*refs):
    place = read(refs[0])
    len_ref, rows, inverse = refs[1:4]
    parts = refs[4:14]
    out_a, out_b, held, heads, sem = refs[14:]
    copies = weight_copies(place, parts, held, sem)
    start_all(copies)
    wait_all(copies)

    @pl.loop(0, 6)
    def _(n):
        here = pl.ds(pl.multiple_of(lax.div(n, 3) * PLEN, PLEN), PLEN)
        there = pl.ds(pl.multiple_of(lax.rem(n, 3) * HD, HD), HD)
        total = jnp.dot(rows[here, :], held[:, there], preferred_element_type=jnp.float32)
        heads[here, there] = (total * inverse[here, :]).astype(jnp.bfloat16)

    for p, out in enumerate((out_a, out_b)):
        here = pl.ds(p * PLEN, PLEN)
        query, key, value = (heads[here, i * HD : (i + 1) * HD] for i in range(3))
        scores = lax.dot_general(
            query, key, (((1,), (1,)), ((), ())), preferred_element_type=jnp.float32
        ) * HD ** (-0.5)
        slot = lax.broadcasted_iota(jnp.int32, (PLEN, PLEN), 1)
        scores = jnp.where(slot < len_ref[p], scores, masked_score)
        expon = jnp.exp(scores - jnp.max(scores, axis=-1, keepdims=True))
        probs = (expon / jnp.sum(expon, axis=-1, keepdims=True)).astype(jnp.bfloat16)
        out[...] = jnp.dot(probs, value, preferred_element_type=jnp.float32).astype(jnp.bfloat16)


def residual_kernel(*refs):
    place = read(refs[0])
    parts, weights, embedded = refs[1:6], refs[6:16], refs[16]
    out, rows, held, sem, weight_sem = refs[17:]
    copies = weight_copies(place, weights, held, weight_sem) + row_copies(place, parts, rows, sem)
    start_all(copies)
    wait_all(copies)
    total = jnp.dot(rows[...], held[...], preferred_element_type=jnp.float32)
    out[...] = (embedded[...].astype(jnp.float32) + total).astype(jnp.bfloat16)


def cross_kernel(p, *refs):
    place = read(refs[0])
    parts, weights, gain_row = refs[1:6], refs[6:16], refs[16]
    keys, values, rows, held, heads, inverse, sem, weight_sem, out_sem = refs[-9:]
    loads = weight_copies(place, weights, held, weight_sem)
    copies = row_copies(place, parts, rows, sem)
    start_all(copies + loads)
    wait_all(copies)
    scale_rows(rows, gain_row, inverse)
    wait_all(loads)

    @pl.loop(0, 2)
    def _(n):
        there = pl.ds(pl.multiple_of(n * HD, HD), HD)
        total = jnp.dot(rows[...], held[:, there], preferred_element_type=jnp.float32)
        heads[n] = (total * inverse[...]).astype(jnp.bfloat16)

    here = pl.ds(p * PLEN, PLEN)
    stores = [
        pltpu.make_async_copy(heads.at[n], out.at[here], out_sem.at[n])
        for n, out in enumerate((keys, values))
    ]
    start_all(stores)
    wait_all(stores)


def bf16(*shape):
    return jax.ShapeDtypeStruct(shape, jnp.bfloat16)


def f32(*shape):
    return jax.ShapeDtypeStruct(shape, jnp.float32)


def call(kernel, outs, ins, scratch, flops, moved, out_spec=VMEM, aliases=()):
    return pl.pallas_call(
        kernel,
        out_shape=outs,
        in_specs=ins,
        out_specs=jax.tree.map(lambda _: out_spec, outs),
        input_output_aliases=dict(aliases),
        scratch_shapes=scratch,
        compiler_params=pltpu.CompilerParams(vmem_limit_bytes=28 << 20),
        cost_estimate=pl.CostEstimate(flops=flops, bytes_accessed=moved, transcendentals=0),
    )


def vmem(*shape, kind=jnp.bfloat16):
    return pltpu.VMEM(shape, kind)


def body(
    token_ids,
    passage_lengths,
    embedding,
    attn_gain,
    final_gain,
    query_weight,
    key_weight,
    value_weight,
    out_weight,
    crosskey_weight,
    crossvalue_weight,
):
    tokens = 2 * PLEN
    dma = pltpu.SemaphoreType.DMA((BLOCKS,))
    place = jnp.stack([lax.axis_index("row"), lax.axis_index("col")]).astype(jnp.int32)
    qkv_weight = jnp.concatenate([query_weight, key_weight, value_weight], axis=1)
    cross_weight = jnp.concatenate([crosskey_weight, crossvalue_weight], axis=1)
    early = gather_weight(qkv_weight)
    embedded = embedding.at[token_ids.reshape(-1)].get(mode="promise_in_bounds")
    gains = jnp.concatenate(
        [attn_gain[None, :], final_gain[None, :], jnp.zeros((GAIN_ROWS - 2, HD), jnp.bfloat16)],
        axis=0,
    )
    chunk = jnp.concatenate([embedded, gains], axis=0)
    parts = gather_direct(chunk)
    rows, inverse, final_row = call(
        prepare_kernel,
        (bf16(tokens, D), f32(tokens, 1), f32(1, D)),
        [SMEM] + [ANY] * 4,
        [vmem(GAIN_ROWS, D), vmem(1, D, kind=jnp.float32), dma, dma],
        100 * tokens * D * D // 16,
        8 << 20,
    )(place, *parts)
    attended = call(
        attend_kernel,
        (bf16(PLEN, HD), bf16(PLEN, HD)),
        [SMEM, SMEM, VMEM, VMEM] + [ANY] * 10,
        [vmem(D, 3 * HD), vmem(tokens, 3 * HD), dma],
        2 * tokens * D * 3 * HD,
        10 << 20,
    )(place, passage_lengths, rows, inverse, *early)
    outer = gather_weight(out_weight)
    cross = gather_weight(cross_weight)
    hidden = []
    for p in range(2):
        parts = gather_halved(attended[p])
        hidden.append(
            call(
                residual_kernel,
                bf16(PLEN, HD),
                [SMEM] + [ANY] * 15 + [VMEM],
                [vmem(PLEN, D), vmem(D, HD), dma, dma],
                2 * PLEN * D * HD,
                4 << 20,
            )(place, *parts, *outer, embedded[p * PLEN : (p + 1) * PLEN])
        )
    crossed = ()
    for p in range(2):
        parts = gather_halved(hidden[p])
        crossed = call(
            functools.partial(cross_kernel, p),
            (bf16(tokens, HD), bf16(tokens, HD)),
            [SMEM] + [ANY] * 15 + [VMEM] + [ANY] * len(crossed),
            [
                vmem(PLEN, D),
                vmem(D, 2 * HD),
                vmem(2, PLEN, HD),
                vmem(PLEN, 1, kind=jnp.float32),
                dma,
                dma,
                pltpu.SemaphoreType.DMA((2,)),
            ],
            2 * PLEN * D * 2 * HD,
            6 << 20,
            out_spec=ANY,
            aliases=((17, 0), (18, 1))[: len(crossed)],
        )(place, *parts, *cross, final_row, *crossed)
    keys, values = (part.reshape(tokens, 1, HD) for part in crossed)
    return jnp.concatenate(hidden, axis=0), keys, values


def solution(mesh):
    return jax.shard_map(
        body,
        mesh=mesh,
        in_specs=(
            P("row", None),
            P("row"),
            P(None, "col"),
            P("col"),
            P("col"),
            P("row", "col"),
            P("row", "col"),
            P("row", "col"),
            P("row", "col"),
            P("row", "col"),
            P("row", "col"),
        ),
        out_specs=(P("row", "col"), P("row", "col", None), P("row", "col", None)),
        check_vma=False,
    )
```

```python
import jax
import jax.numpy as jnp
from jax import lax
from jax.experimental import pallas as pl
from jax.experimental.pallas import tpu as pltpu
from jax.sharding import PartitionSpec as P

D = 4096
HD = 256
PLEN = 256
SIDE = 4
BLOCKS = SIDE * SIDE
GAIN_ROWS = 16

epsilon = 1e-06
masked_score = -1000000000.0


ANY = pl.BlockSpec(memory_space=pl.ANY)
SMEM = pl.BlockSpec(memory_space=pltpu.SMEM)
VMEM = pl.BlockSpec(memory_space=pltpu.VMEM)

DEPTH = 8
SHIFTS = (1, 3, 2)
OFFSETS = (0, 3, 1, 2)


def moves(step):
    def index(z, c, x, y):
        return ((z % DEPTH * 2 + c) * SIDE + x % SIDE) * SIDE + y % SIDE

    return [
        (index(z, c, x, y), index(*step(z, c, x, y)))
        for z in range(DEPTH)
        for c in range(2)
        for x in range(SIDE)
        for y in range(SIDE)
    ]


def send(block, step):
    return lax.ppermute(block, ("row", "col"), moves(step))


def first_leg(block, shift):
    return send(block, lambda z, c, x, y: (z, c, x + shift * (1 - c), y + shift * c))


def second_leg(block, shift):
    return send(block, lambda z, c, x, y: (z, c, x + shift * c, y + shift * (1 - c)))


def along_z(block):
    return send(block, lambda z, c, x, y: (z + 1 - 2 * c, c, x, y))


def swap_cores(block):
    return send(block, lambda z, c, x, y: (z, 1 - c, x, y))


def gather_first(chunk):
    return jnp.stack([chunk] + [first_leg(chunk, s) for s in SHIFTS])


def gather_direct(chunk):
    stack = gather_first(chunk)
    return [stack] + [second_leg(stack, s) for s in SHIFTS]


def gather_halved(chunk):
    stack = gather_first(chunk)
    back, ahead = second_leg(stack, 1), second_leg(stack, 3)
    return [stack, back, ahead, second_leg(back[:2], 1), second_leg(ahead[2:], 3)]


def gather_weight(shard, late):
    other = swap_cores(shard)
    block = jnp.stack([shard, other])
    parts = [shard, other]
    hops = []
    for hop in range(1, DEPTH // 2 + 1):
        block = along_z(block if hop < DEPTH // 2 else block[0])
        hops.append(block)
    if late:
        both = jnp.concatenate(hops[:3] + [hops[3][None]])
        return parts + hops + [swap_cores(both)]
    crossed = swap_cores(jnp.concatenate(hops[:3]))
    return parts + hops + [crossed, swap_cores(hops[3])]


def weight_places(place, late):
    z, c = place[0], place[1]
    up = 1 - 2 * c

    def row(depth, core):
        return lax.rem(depth + DEPTH, DEPTH) * 2 + core

    last = DEPTH // 2
    places = [(0, None, row(z, c)), (1, None, row(z, 1 - c))]
    for hop in range(1, last):
        places += [(1 + hop, 0, row(z - hop * up, c)), (1 + hop, 1, row(z - hop * up, 1 - c))]
        spot = 2 * hop - 2
        places += [(6, spot, row(z + hop * up, 1 - c)), (6, spot + 1, row(z + hop * up, c))]
    far = (6, 6) if late else (7, None)
    return places + [(5, None, row(z + last, c)), (*far, row(z + last, 1 - c))]


def weight_copies(place, parts, held, sem):
    copies = []
    for n, (part, spot, row) in enumerate(weight_places(place, len(parts) == 7)):
        source = parts[part] if spot is None else parts[part].at[spot]
        target = held.at[pl.ds(pl.multiple_of(row * HD, HD), HD)]
        copies.append(pltpu.make_async_copy(source, target, sem.at[n]))
    return copies


def block_of(place, first, second):
    c = place[1]
    x = place[2] + OFFSETS[first] * (1 - c) + OFFSETS[second] * c
    y = place[3] + OFFSETS[first] * c + OFFSETS[second] * (1 - c)
    return lax.rem(x, SIDE) * SIDE + lax.rem(y, SIDE)


def row_copies(place, parts, rows, sem, start=0):
    copies = []
    count = rows.shape[0]
    for first in range(SIDE):
        for second in range(SIDE):
            where = pl.ds(pl.multiple_of(block_of(place, first, second) * HD, HD), HD)
            if second < 3 or len(parts) == 4:
                source = parts[second].at[first]
            else:
                source = parts[3 + first // 2].at[first % 2]
            copies.append(
                pltpu.make_async_copy(
                    source.at[pl.ds(start, count)],
                    rows.at[:, where],
                    sem.at[first * SIDE + second],
                )
            )
    return copies


def read(place_ref):
    row, col = place_ref[0], place_ref[1]
    return [lax.div(row, 2), lax.rem(row, 2), lax.div(col, SIDE), lax.rem(col, SIDE)]


def start_all(copies):
    for copy in copies:
        copy.start()


def wait_all(copies):
    for copy in copies:
        copy.wait()


def scale_rows(rows, gain, inverse):
    step, width = 32, 512

    @pl.loop(0, rows.shape[0] // step)
    def _(tile):
        here = pl.ds(pl.multiple_of(tile * step, step), step)
        total = jnp.zeros((step, 128), jnp.float32)
        for part in range(D // width):
            cols = pl.ds(part * width, width)
            wide = rows[here, cols].astype(jnp.float32)
            square = wide * wide
            for lane in range(width // 128):
                total += square[:, lane * 128 : (lane + 1) * 128]
            rows[here, cols] = (wide * gain[:, cols]).astype(jnp.bfloat16)
        mean = jnp.sum(total, axis=1, keepdims=True) / D
        inverse[here, :] = lax.rsqrt(mean + epsilon)


def prepare_kernel(*refs):
    place = read(refs[0])
    parts = refs[1:5]
    rows, inverse, final_ref, gains, gain_row, sem, gain_sem = refs[5:]
    copies = row_copies(place, parts, gains, gain_sem, rows.shape[0]) + row_copies(place, parts, rows, sem)
    start_all(copies)
    wait_all(copies)
    gain_row[...] = gains[0:1, :].astype(jnp.float32)
    final_ref[...] = gains[1:2, :].astype(jnp.float32)
    scale_rows(rows, gain_row, inverse)


def attend_kernel(*refs):
    place = read(refs[0])
    len_ref, rows, inverse = refs[1:4]
    parts = refs[4:12]
    out, held, heads, sem = refs[12:]
    copies = weight_copies(place, parts, held, sem)
    start_all(copies)
    wait_all(copies)

    @pl.loop(0, 6)
    def _(n):
        here = pl.ds(pl.multiple_of(lax.div(n, 3) * PLEN, PLEN), PLEN)
        there = pl.ds(pl.multiple_of(lax.rem(n, 3) * HD, HD), HD)
        total = jnp.dot(rows[here, :], held[:, there], preferred_element_type=jnp.float32)
        heads[here, there] = (total * inverse[here, :]).astype(jnp.bfloat16)

    for p in range(2):
        here = pl.ds(p * PLEN, PLEN)
        query, key, value = (heads[here, i * HD : (i + 1) * HD] for i in range(3))
        scores = lax.dot_general(
            query, key, (((1,), (1,)), ((), ())), preferred_element_type=jnp.float32
        ) * HD ** (-0.5)
        slot = lax.broadcasted_iota(jnp.int32, (PLEN, PLEN), 1)
        scores = jnp.where(slot < len_ref[p], scores, masked_score)
        expon = jnp.exp(scores - jnp.max(scores, axis=-1, keepdims=True))
        probs = (expon / jnp.sum(expon, axis=-1, keepdims=True)).astype(jnp.bfloat16)
        out[here, :] = jnp.dot(probs, value, preferred_element_type=jnp.float32).astype(jnp.bfloat16)


def residual_kernel(*refs):
    place = read(refs[0])
    parts, weights, embedded = refs[1:6], refs[6:13], refs[13]
    out, rows, held, sem, weight_sem = refs[14:]
    copies = weight_copies(place, weights, held, weight_sem) + row_copies(place, parts, rows, sem)
    start_all(copies)
    wait_all(copies)
    total = jnp.dot(rows[...], held[...], preferred_element_type=jnp.float32)
    out[...] = (embedded[...].astype(jnp.float32) + total).astype(jnp.bfloat16)


def cross_kernel(*refs):
    place = read(refs[0])
    parts, weights, gain_row = refs[1:6], refs[6:13], refs[13]
    keys, values, rows, held, heads, inverse, sem, weight_sem, out_sem = refs[14:]
    loads = weight_copies(place, weights, held, weight_sem)
    copies = row_copies(place, parts, rows, sem)
    start_all(copies + loads)
    wait_all(copies)
    scale_rows(rows, gain_row, inverse)
    wait_all(loads)
    stores = []
    for n, out in enumerate((keys, values)):
        total = jnp.dot(rows[...], held[:, n * HD : (n + 1) * HD], preferred_element_type=jnp.float32)
        heads[n] = (total * inverse[...]).astype(jnp.bfloat16)
        stores.append(pltpu.make_async_copy(heads.at[n], out, out_sem.at[n]))
        stores[n].start()
    wait_all(stores)


def bf16(*shape):
    return jax.ShapeDtypeStruct(shape, jnp.bfloat16)


def f32(*shape):
    return jax.ShapeDtypeStruct(shape, jnp.float32)


def call(kernel, outs, ins, scratch, flops, moved, out_spec=VMEM):
    return pl.pallas_call(
        kernel,
        out_shape=outs,
        in_specs=ins,
        out_specs=jax.tree.map(lambda _: out_spec, outs),
        scratch_shapes=scratch,
        compiler_params=pltpu.CompilerParams(vmem_limit_bytes=28 << 20),
        cost_estimate=pl.CostEstimate(flops=flops, bytes_accessed=moved, transcendentals=0),
    )


def join_kernel(*refs):
    parts, out, sem = refs[:-2], refs[-2], refs[-1]
    copies = [
        pltpu.make_async_copy(part, out.at[:, pl.ds(n * HD, HD)], sem.at[n]) for n, part in enumerate(parts)
    ]
    start_all(copies)
    wait_all(copies)


def side_by_side(*shards):
    return call(
        join_kernel,
        bf16(HD, len(shards) * HD),
        [ANY] * len(shards),
        [pltpu.SemaphoreType.DMA((len(shards),))],
        0,
        len(shards) << 17,
    )(*shards)


def vmem(*shape, kind=jnp.bfloat16):
    return pltpu.VMEM(shape, kind)


def body(
    token_ids,
    passage_lengths,
    embedding,
    attn_gain,
    final_gain,
    query_weight,
    key_weight,
    value_weight,
    out_weight,
    crosskey_weight,
    crossvalue_weight,
):
    tokens = 2 * PLEN
    dma = pltpu.SemaphoreType.DMA((BLOCKS,))
    place = jnp.stack([lax.axis_index("row"), lax.axis_index("col")]).astype(jnp.int32)
    qkv_weight = side_by_side(query_weight, key_weight, value_weight)
    cross_weight = side_by_side(crosskey_weight, crossvalue_weight)
    early = gather_weight(qkv_weight, False)
    embedded = embedding.at[token_ids.reshape(-1)].get(mode="promise_in_bounds")
    gains = jnp.concatenate(
        [attn_gain[None, :], final_gain[None, :], jnp.zeros((GAIN_ROWS - 2, HD), jnp.bfloat16)],
        axis=0,
    )
    chunk = jnp.concatenate([embedded, gains], axis=0)
    parts = gather_direct(chunk)
    rows, inverse, final_row = call(
        prepare_kernel,
        (bf16(tokens, D), f32(tokens, 1), f32(1, D)),
        [SMEM] + [ANY] * 4,
        [vmem(GAIN_ROWS, D), vmem(1, D, kind=jnp.float32), dma, dma],
        100 * tokens * D * D // 16,
        8 << 20,
    )(place, *parts)
    attended = call(
        attend_kernel,
        bf16(tokens, HD),
        [SMEM, SMEM, VMEM, VMEM] + [ANY] * 8,
        [vmem(D, 3 * HD), vmem(tokens, 3 * HD), dma],
        2 * tokens * D * 3 * HD,
        10 << 20,
    )(place, passage_lengths, rows, inverse, *early)
    outer = gather_weight(out_weight, True)
    cross = gather_weight(cross_weight, True)
    parts = gather_halved(attended)
    hidden = call(
        residual_kernel,
        bf16(tokens, HD),
        [SMEM] + [ANY] * 12 + [VMEM],
        [vmem(tokens, D), vmem(D, HD), dma, dma],
        2 * tokens * D * HD,
        6 << 20,
    )(place, *parts, *outer, embedded)
    parts = gather_halved(hidden)
    keys, values = call(
        cross_kernel,
        (bf16(tokens, HD), bf16(tokens, HD)),
        [SMEM] + [ANY] * 12 + [VMEM],
        [
            vmem(tokens, D),
            vmem(D, 2 * HD),
            vmem(2, tokens, HD),
            vmem(tokens, 1, kind=jnp.float32),
            dma,
            dma,
            pltpu.SemaphoreType.DMA((2,)),
        ],
        2 * tokens * D * 2 * HD,
        8 << 20,
        out_spec=ANY,
    )(place, *parts, *cross, final_row)
    return hidden, keys.reshape(tokens, 1, HD), values.reshape(tokens, 1, HD)


def solution(mesh):
    return jax.shard_map(
        body,
        mesh=mesh,
        in_specs=(
            P("row", None),
            P("row"),
            P(None, "col"),
            P("col"),
            P("col"),
            P("row", "col"),
            P("row", "col"),
            P("row", "col"),
            P("row", "col"),
            P("row", "col"),
            P("row", "col"),
        ),
        out_specs=(P("row", "col"), P("row", "col", None), P("row", "col", None)),
        check_vma=False,
    )
```

```python
import jax
import jax.numpy as jnp
from jax import lax
from jax.experimental import pallas as pl
from jax.experimental.pallas import tpu as pltpu
from jax.sharding import PartitionSpec as P

D = 4096
HD = 256
PLEN = 256
SIDE = 4
BLOCKS = SIDE * SIDE
GAIN_ROWS = 16

epsilon = 1e-06
masked_score = -1000000000.0


ANY = pl.BlockSpec(memory_space=pl.ANY)
SMEM = pl.BlockSpec(memory_space=pltpu.SMEM)
VMEM = pl.BlockSpec(memory_space=pltpu.VMEM)
HBM = pl.BlockSpec(memory_space=pltpu.HBM)

DEPTH = 8
SHIFTS = (1, 3, 2)
OFFSETS = (0, 3, 1, 2)


def moves(step):
    def index(z, c, x, y):
        return ((z % DEPTH * 2 + c) * SIDE + x % SIDE) * SIDE + y % SIDE

    return [
        (index(z, c, x, y), index(*step(z, c, x, y)))
        for z in range(DEPTH)
        for c in range(2)
        for x in range(SIDE)
        for y in range(SIDE)
    ]


def send(block, step):
    return lax.ppermute(block, ("row", "col"), moves(step))


def first_leg(block, shift):
    return send(block, lambda z, c, x, y: (z, c, x + shift * (1 - c), y + shift * c))


def second_leg(block, shift):
    return send(block, lambda z, c, x, y: (z, c, x + shift * c, y + shift * (1 - c)))


def along_z(block):
    return send(block, lambda z, c, x, y: (z + 1 - 2 * c, c, x, y))


def swap_cores(block):
    return send(block, lambda z, c, x, y: (z, 1 - c, x, y))


def gather_first(chunk):
    return jnp.stack([chunk] + [first_leg(chunk, s) for s in SHIFTS])


def gather_direct(chunk):
    stack = gather_first(chunk)
    return [stack] + [second_leg(stack, s) for s in SHIFTS]


def gather_halved(chunk):
    stack = gather_first(chunk)
    back, ahead = second_leg(stack, 1), second_leg(stack, 3)
    return [stack, back, ahead, second_leg(back[:2], 1), second_leg(ahead[2:], 3)]


def gather_weight(shard, other, late):
    block = jnp.stack([shard, other])
    parts = [shard, other]
    hops = []
    for hop in range(1, DEPTH // 2 + 1):
        block = along_z(block if hop < DEPTH // 2 else block[0])
        hops.append(block)
    if late:
        both = jnp.concatenate(hops[:3] + [hops[3][None]])
        return parts + hops + [swap_cores(both)]
    crossed = swap_cores(jnp.concatenate(hops[:3]))
    return parts + hops + [crossed, swap_cores(hops[3])]


def arrival(place, row):
    z, c = place[0], place[1]
    away = lax.rem((lax.div(row, 2) - z) * (1 - 2 * c) + DEPTH, DEPTH)
    same = jnp.where(lax.rem(row, 2) == c, 1, 0)
    near = jnp.where(away == 0, 1 - same, 14 + 1 - same)
    behind = 2 + 2 * (DEPTH - 1 - away) + 1 - same
    ahead = 8 + 2 * (away - 1) + same
    half = DEPTH // 2
    inner = jnp.where(away > half, behind, ahead)
    return jnp.where((away == 0) | (away == half), near, inner)


def late_places(place):
    z, c = place[0], place[1]
    up = 1 - 2 * c

    def row(depth, core):
        return lax.rem(depth + DEPTH, DEPTH) * 2 + core

    last = DEPTH // 2
    places = [(0, None, row(z, c)), (1, None, row(z, 1 - c))]
    for hop in range(1, last):
        places += [(1 + hop, 0, row(z - hop * up, c)), (1 + hop, 1, row(z - hop * up, 1 - c))]
        spot = 2 * hop - 2
        places += [(6, spot, row(z + hop * up, 1 - c)), (6, spot + 1, row(z + hop * up, c))]
    return places + [(5, None, row(z + last, c)), (6, 6, row(z + last, 1 - c))]


def gather_spot(place, row):
    c = place[1]
    away_x = lax.rem(lax.div(row, SIDE) - place[2] + SIDE, SIDE)
    away_y = lax.rem(lax.rem(row, SIDE) - place[3] + SIDE, SIDE)

    def index(away):
        return jnp.where(away == 0, 0, jnp.where(away == 3, 1, away + 1))

    first = index(away_x * (1 - c) + away_y * c)
    second = index(away_x * c + away_y * (1 - c))
    return second * SIDE + first


def block_of(place, first, second):
    c = place[1]
    x = place[2] + OFFSETS[first] * (1 - c) + OFFSETS[second] * c
    y = place[3] + OFFSETS[first] * c + OFFSETS[second] * (1 - c)
    return lax.rem(x, SIDE) * SIDE + lax.rem(y, SIDE)


def read(place_ref):
    row, col = place_ref[0], place_ref[1]
    return [lax.div(row, 2), lax.rem(row, 2), lax.div(col, SIDE), lax.rem(col, SIDE)]


def start_all(copies):
    for copy in copies:
        copy.start()


def wait_all(copies):
    for copy in copies:
        copy.wait()


def lanes(square):
    return sum(square[:, n * 128 : (n + 1) * 128] for n in range(square.shape[1] // 128))


def prepare_kernel(place_ref, own, back, ahead, far, rows, square, final_ref):
    place = read(place_ref)
    tokens, step = rows.shape[0], 64
    for second, part in enumerate((own, back, ahead, far)):
        for first in range(SIDE):
            spot = arrival(place, block_of(place, first, second))
            there = pl.ds(pl.multiple_of(spot * HD, HD), HD)
            gains = part[first, pl.ds(tokens, GAIN_ROWS), :].astype(jnp.float32)
            final_ref[second * SIDE + first] = gains[1:2, :]
            gain = gains[0:1, :]

            @pl.loop(0, tokens // step)
            def _(tile):
                here = pl.ds(pl.multiple_of(tile * step, step), step)
                wide = part[first, here, :].astype(jnp.float32)
                total = lanes(wide * wide)
                square[here, :] = total if second + first == 0 else square[here, :] + total
                rows[here, there] = (wide * gain).astype(jnp.bfloat16)


def weight_loads(sources, held, sem):
    copies, at = [], 0
    for n, source in enumerate(sources):
        if len(source.shape) == 2:
            copies.append(pltpu.make_async_copy(source, held.at[at], sem.at[n]))
            at += 1
        else:
            count = source.shape[0]
            copies.append(pltpu.make_async_copy(source, held.at[pl.ds(at, count)], sem.at[n]))
            at += count
    return copies


def project_kernel(rows, own, other, hop1, hop2, hop3, crossed, total, held, sem):
    copies = weight_loads((own, other, hop1, hop2, hop3, crossed), held, sem)
    start_all(copies)
    wait_all(copies)
    weight = held.reshape(14 * HD, 3 * HD)

    @pl.loop(0, 6)
    def _(n):
        here = pl.ds(pl.multiple_of(lax.div(n, 3) * PLEN, PLEN), PLEN)
        there = pl.ds(pl.multiple_of(lax.rem(n, 3) * HD, HD), HD)
        total[here, there] = jnp.dot(
            rows[here, : 14 * HD], weight[:, there], preferred_element_type=jnp.float32
        )


def attend_kernel(len_ref, rows, square, total, far, far_crossed, out, heads):
    @pl.loop(0, 2)
    def _(p):
        here = pl.ds(pl.multiple_of(p * PLEN, PLEN), PLEN)
        mean = jnp.sum(square[here, :], axis=1, keepdims=True) / D
        inverse = lax.rsqrt(mean + epsilon)
        for n in range(3):
            there = pl.ds(n * HD, HD)
            head = total[here, there]
            head += jnp.dot(rows[here, 14 * HD : 15 * HD], far[:, there], preferred_element_type=jnp.float32)
            head += jnp.dot(rows[here, 15 * HD :], far_crossed[:, there], preferred_element_type=jnp.float32)
            heads[n] = (head * inverse).astype(jnp.bfloat16)
        scores = lax.dot_general(
            heads[0], heads[1], (((1,), (1,)), ((), ())), preferred_element_type=jnp.float32
        ) * HD ** (-0.5)
        slot = lax.broadcasted_iota(jnp.int32, (PLEN, PLEN), 1)
        scores = jnp.where(slot < len_ref[p], scores, masked_score)
        expon = jnp.exp(scores - jnp.max(scores, axis=-1, keepdims=True))
        probs = (expon / jnp.sum(expon, axis=-1, keepdims=True)).astype(jnp.bfloat16)
        out[here, :] = jnp.dot(probs, heads[2], preferred_element_type=jnp.float32).astype(jnp.bfloat16)


def arrange_kernel(*refs):
    place = read(refs[0])
    parts, out, sem = refs[1:8], refs[8], refs[9]
    copies = []
    for n, (part, spot, row) in enumerate(late_places(place)):
        source = parts[part] if spot is None else parts[part].at[spot]
        copies.append(pltpu.make_async_copy(source, out.at[gather_spot(place, row)], sem.at[n]))
    start_all(copies)
    wait_all(copies)


def residual_near_kernel(own, back, ahead, weight, embedded, total):
    @pl.loop(0, 2)
    def _(p):
        here = pl.ds(pl.multiple_of(p * PLEN, PLEN), PLEN)
        sum_here = embedded[here, :].astype(jnp.float32)
        for k in range(12):
            part = (own, back, ahead)[k // SIDE]
            sum_here += jnp.dot(part[k % SIDE, here, :], weight[k], preferred_element_type=jnp.float32)
        total[here, :] = sum_here


def residual_far_kernel(far_back, far_ahead, weight, total, out, held, sem):
    load = pltpu.make_async_copy(weight.at[pl.ds(12, 4)], held, sem)
    load.start()
    load.wait()

    @pl.loop(0, 2)
    def _(p):
        here = pl.ds(pl.multiple_of(p * PLEN, PLEN), PLEN)
        sum_here = total[here, :]
        for k in range(SIDE):
            part = (far_back, far_ahead)[k // 2]
            sum_here += jnp.dot(part[k % 2, here, :], held[k], preferred_element_type=jnp.float32)
        out[here, :] = sum_here.astype(jnp.bfloat16)


def scaled(block, gain):
    wide = block.astype(jnp.float32)
    return (wide * gain).astype(jnp.bfloat16), lanes(wide * wide)


def cross_near_kernel(own, back, ahead, weight, gains, total, square):
    @pl.loop(0, 4)
    def _(p):
        here = pl.ds(pl.multiple_of(p * 128, 128), 128)
        for k in range(12):
            part = (own, back, ahead)[k // SIDE]
            block, squares = scaled(part[k % SIDE, here, :], gains[k])
            term = jnp.dot(block, weight[k], preferred_element_type=jnp.float32)
            total[here, :] = term if k == 0 else total[here, :] + term
            square[here, :] = squares if k == 0 else square[here, :] + squares


def cross_far_kernel(far_back, far_ahead, weight, gains, total, square, keys, values, held, sem):
    load = pltpu.make_async_copy(weight.at[pl.ds(12, 4)], held, sem)
    load.start()
    load.wait()

    @pl.loop(0, 4)
    def _(p):
        here = pl.ds(pl.multiple_of(p * 128, 128), 128)
        sum_here, squares = total[here, :], square[here, :]
        for k in range(SIDE):
            part = (far_back, far_ahead)[k // 2]
            block, more = scaled(part[k % 2, here, :], gains[12 + k])
            sum_here += jnp.dot(block, held[k], preferred_element_type=jnp.float32)
            squares += more
        inverse = lax.rsqrt(jnp.sum(squares, axis=1, keepdims=True) / D + epsilon)
        head = (sum_here * inverse).astype(jnp.bfloat16)
        keys[here, :] = head[:, :HD]
        values[here, :] = head[:, HD:]


def bf16(*shape):
    return jax.ShapeDtypeStruct(shape, jnp.bfloat16)


def f32(*shape):
    return jax.ShapeDtypeStruct(shape, jnp.float32)


def call(kernel, outs, ins, scratch, flops, moved, grant=28):
    return pl.pallas_call(
        kernel,
        out_shape=outs,
        in_specs=ins,
        out_specs=jax.tree.map(lambda _: VMEM, outs),
        scratch_shapes=scratch,
        compiler_params=pltpu.CompilerParams(vmem_limit_bytes=grant << 20),
        cost_estimate=pl.CostEstimate(flops=flops, bytes_accessed=moved, transcendentals=0),
    )


def pack_kernel(embedded, attn_gain, final_gain, out):
    tokens = embedded.shape[0]
    out[pl.ds(0, tokens), :] = embedded[...]
    place = lax.broadcasted_iota(jnp.int32, (GAIN_ROWS, HD), 0)
    first = jnp.broadcast_to(attn_gain[...].astype(jnp.float32).reshape(1, HD), (GAIN_ROWS, HD))
    second = jnp.broadcast_to(final_gain[...].astype(jnp.float32).reshape(1, HD), (GAIN_ROWS, HD))
    both = jnp.where(place == 0, first, jnp.where(place == 1, second, 0.0))
    out[pl.ds(tokens, GAIN_ROWS), :] = both.astype(jnp.bfloat16)


def join_kernel(*refs):
    parts, out, sem = refs[:-2], refs[-2], refs[-1]
    copies = [
        pltpu.make_async_copy(part, out.at[:, pl.ds(n * HD, HD)], sem.at[n]) for n, part in enumerate(parts)
    ]
    start_all(copies)
    wait_all(copies)


def side_by_side(*shards):
    return call(
        join_kernel,
        bf16(HD, len(shards) * HD),
        [HBM] * len(shards),
        [pltpu.SemaphoreType.DMA((len(shards),))],
        0,
        len(shards) << 17,
        grant=60,
    )(*shards)


def vmem(*shape, kind=jnp.bfloat16):
    return pltpu.VMEM(shape, kind)


def body(
    token_ids,
    passage_lengths,
    embedding,
    attn_gain,
    final_gain,
    query_weight,
    key_weight,
    value_weight,
    out_weight,
    crosskey_weight,
    crossvalue_weight,
):
    tokens = 2 * PLEN
    dma = pltpu.SemaphoreType.DMA((BLOCKS,))
    place = jnp.stack([lax.axis_index("row"), lax.axis_index("col")]).astype(jnp.int32)
    qkv_weight = side_by_side(query_weight, key_weight, value_weight)
    qkv_other = swap_cores(qkv_weight)
    early = gather_weight(qkv_weight, qkv_other, False)
    embedded = embedding.at[token_ids.reshape(-1)].get(mode="promise_in_bounds")
    chunk = call(
        pack_kernel, bf16(tokens + GAIN_ROWS, HD), [VMEM] * 3, [], 0, 1 << 19
    )(embedded, attn_gain, final_gain)
    parts = gather_direct(chunk)
    rows, square, gains = call(
        prepare_kernel,
        (bf16(tokens, D), f32(tokens, 128), f32(BLOCKS, 1, HD)),
        [SMEM] + [VMEM] * 4,
        [],
        100 * tokens * D * D // 16,
        8 << 20,
    )(place, *parts)
    total = call(
        project_kernel,
        f32(tokens, 3 * HD),
        [VMEM] + [ANY] * 6,
        [vmem(14, HD, 3 * HD), pltpu.SemaphoreType.DMA((6,))],
        2 * tokens * D * 3 * HD,
        10 << 20,
    )(rows, *early[:5], early[6])
    attended = call(
        attend_kernel,
        bf16(tokens, HD),
        [SMEM] + [VMEM] * 5,
        [vmem(3, PLEN, HD)],
        tokens * D * HD,
        4 << 20,
    )(passage_lengths, rows, square, total, early[5], early[7])
    late_weight = side_by_side(out_weight, crosskey_weight, crossvalue_weight)
    late_other = swap_cores(late_weight)
    outer = gather_weight(out_weight, late_other[:, :HD], True)
    cross = gather_weight(late_weight[:, HD:], late_other[:, HD:], True)

    def arrange(weight):
        width = weight[0].shape[1]
        return call(
            arrange_kernel, bf16(BLOCKS, HD, width), [SMEM] + [ANY] * 7, [dma], 0, 4 * D * width
        )(place, *weight)

    parts = gather_halved(attended)
    weight = arrange(outer)
    total = call(
        residual_near_kernel, f32(tokens, HD), [VMEM] * 5, [], 2 * tokens * D * HD, 6 << 20
    )(*parts[:3], weight, embedded)
    hidden = call(
        residual_far_kernel,
        bf16(tokens, HD),
        [VMEM, VMEM, ANY, VMEM],
        [vmem(SIDE, HD, HD), pltpu.SemaphoreType.DMA],
        tokens * D * HD // 2,
        2 << 20,
    )(*parts[3:], weight, total)
    parts = gather_halved(hidden)
    weight = arrange(cross)
    total, square = call(
        cross_near_kernel,
        (f32(tokens, 2 * HD), f32(tokens, 128)),
        [VMEM] * 5,
        [],
        4 * tokens * D * HD,
        8 << 20,
    )(*parts[:3], weight, gains)
    keys, values = call(
        cross_far_kernel,
        (bf16(tokens, HD), bf16(tokens, HD)),
        [VMEM, VMEM, ANY] + [VMEM] * 3,
        [vmem(SIDE, HD, 2 * HD), pltpu.SemaphoreType.DMA],
        tokens * D * HD,
        3 << 20,
    )(*parts[3:], weight, gains, total, square)
    return hidden, keys.reshape(tokens, 1, HD), values.reshape(tokens, 1, HD)


def solution(mesh):
    return jax.shard_map(
        body,
        mesh=mesh,
        in_specs=(
            P("row", None),
            P("row"),
            P(None, "col"),
            P("col"),
            P("col"),
            P("row", "col"),
            P("row", "col"),
            P("row", "col"),
            P("row", "col"),
            P("row", "col"),
            P("row", "col"),
        ),
        out_specs=(P("row", "col"), P("row", "col", None), P("row", "col", None)),
        check_vma=False,
    )
```

```python
import jax
import jax.numpy as jnp
from jax import lax
from jax.experimental import pallas as pl
from jax.experimental.pallas import tpu as pltpu
from jax.sharding import PartitionSpec as P

D = 4096
HD = 256
PLEN = 256
SIDE = 4
BLOCKS = SIDE * SIDE
GAIN_ROWS = 16

epsilon = 1e-06
masked_score = -1000000000.0


ANY = pl.BlockSpec(memory_space=pl.ANY)
SMEM = pl.BlockSpec(memory_space=pltpu.SMEM)
VMEM = pl.BlockSpec(memory_space=pltpu.VMEM)
HBM = pl.BlockSpec(memory_space=pltpu.HBM)

DEPTH = 8
SHIFTS = (1, 3, 2)
OFFSETS = (0, 3, 1, 2)


def moves(step):
    def index(z, c, x, y):
        return ((z % DEPTH * 2 + c) * SIDE + x % SIDE) * SIDE + y % SIDE

    return [
        (index(z, c, x, y), index(*step(z, c, x, y)))
        for z in range(DEPTH)
        for c in range(2)
        for x in range(SIDE)
        for y in range(SIDE)
    ]


def send(block, step):
    return lax.ppermute(block, ("row", "col"), moves(step))


def first_leg(block, shift):
    return send(block, lambda z, c, x, y: (z, c, x + shift * (1 - c), y + shift * c))


def second_leg(block, shift):
    return send(block, lambda z, c, x, y: (z, c, x + shift * c, y + shift * (1 - c)))


def along_z(block):
    return send(block, lambda z, c, x, y: (z + 1 - 2 * c, c, x, y))


def swap_cores(block):
    return send(block, lambda z, c, x, y: (z, 1 - c, x, y))


def gather_first(chunk):
    return jnp.stack([chunk] + [first_leg(chunk, s) for s in SHIFTS])


def gather_direct(chunk):
    stack = gather_first(chunk)
    return [stack] + [second_leg(stack, s) for s in SHIFTS]


def gather_split(chunk):
    back, ahead, far = (first_leg(chunk, s) for s in SHIFTS)
    low, high = jnp.stack([chunk, back]), jnp.stack([ahead, far])
    back_low, ahead_high = second_leg(low, 1), second_leg(high, 3)
    back_high, ahead_low = second_leg(high, 1), second_leg(low, 3)
    passed = [second_leg(back_low, 1), second_leg(ahead_high, 3)]
    return [low, high, back_low, back_high, ahead_low, ahead_high], passed


def gather_weight(shard, other, late):
    block = jnp.stack([shard, other])
    parts = [shard, other]
    hops = []
    for hop in range(1, DEPTH // 2 + 1):
        block = along_z(block if hop < DEPTH // 2 else block[0])
        hops.append(block)
    if late:
        both = jnp.concatenate(hops[:3] + [hops[3][None]])
        return parts + hops + [swap_cores(both)]
    crossed = swap_cores(jnp.concatenate(hops[:3]))
    return parts + hops + [crossed, swap_cores(hops[3])]


def arrival(place, row):
    z, c = place[0], place[1]
    away = lax.rem((lax.div(row, 2) - z) * (1 - 2 * c) + DEPTH, DEPTH)
    same = jnp.where(lax.rem(row, 2) == c, 1, 0)
    near = jnp.where(away == 0, 1 - same, 14 + 1 - same)
    behind = 2 + 2 * (DEPTH - 1 - away) + 1 - same
    ahead = 8 + 2 * (away - 1) + same
    half = DEPTH // 2
    inner = jnp.where(away > half, behind, ahead)
    return jnp.where((away == 0) | (away == half), near, inner)


def late_places(place):
    z, c = place[0], place[1]
    up = 1 - 2 * c

    def row(depth, core):
        return lax.rem(depth + DEPTH, DEPTH) * 2 + core

    last = DEPTH // 2
    places = [(0, None, row(z, c)), (1, None, row(z, 1 - c))]
    for hop in range(1, last):
        places += [(1 + hop, 0, row(z - hop * up, c)), (1 + hop, 1, row(z - hop * up, 1 - c))]
        spot = 2 * hop - 2
        places += [(6, spot, row(z + hop * up, 1 - c)), (6, spot + 1, row(z + hop * up, c))]
    return places + [(5, None, row(z + last, c)), (6, 6, row(z + last, 1 - c))]


def gather_spot(place, row):
    c = place[1]
    away_x = lax.rem(lax.div(row, SIDE) - place[2] + SIDE, SIDE)
    away_y = lax.rem(lax.rem(row, SIDE) - place[3] + SIDE, SIDE)

    def index(away):
        return jnp.where(away == 0, 0, jnp.where(away == 3, 1, away + 1))

    first = index(away_x * (1 - c) + away_y * c)
    second = index(away_x * c + away_y * (1 - c))
    return second * SIDE + first


def block_of(place, first, second):
    c = place[1]
    away = jnp.where(first == 0, 0, jnp.where(first == 1, 3, first - 1))
    x = place[2] + away * (1 - c) + OFFSETS[second] * c
    y = place[3] + away * c + OFFSETS[second] * (1 - c)
    return lax.rem(x, SIDE) * SIDE + lax.rem(y, SIDE)


def read(place_ref):
    row, col = place_ref[0], place_ref[1]
    return [lax.div(row, 2), lax.rem(row, 2), lax.div(col, SIDE), lax.rem(col, SIDE)]


def start_all(copies):
    for copy in copies:
        copy.start()


def wait_all(copies):
    for copy in copies:
        copy.wait()


def lanes(square):
    return sum(square[:, n * 128 : (n + 1) * 128] for n in range(square.shape[1] // 128))


def prepare_kernel(place_ref, own, back, ahead, far, rows, square, final_ref):
    place = read(place_ref)
    tokens, step = rows.shape[0], 64
    square[...] = jnp.zeros_like(square)
    for second, part in enumerate((own, back, ahead, far)):

        @pl.loop(0, SIDE)
        def _(first):
            spot = arrival(place, block_of(place, first, second))
            there = pl.ds(pl.multiple_of(spot * HD, HD), HD)
            gains = part[first, pl.ds(tokens, GAIN_ROWS), :].astype(jnp.float32)
            final_ref[second * SIDE + first] = gains[1:2, :]
            gain = gains[0:1, :]

            @pl.loop(0, tokens // step)
            def _(tile):
                here = pl.ds(pl.multiple_of(tile * step, step), step)
                wide = part[first, here, :].astype(jnp.float32)
                square[here, :] += lanes(wide * wide)
                rows[here, there] = (wide * gain).astype(jnp.bfloat16)


def weight_loads(sources, held, sem):
    copies, at = [], 0
    for n, source in enumerate(sources):
        if len(source.shape) == 2:
            copies.append(pltpu.make_async_copy(source, held.at[at], sem.at[n]))
            at += 1
        else:
            count = source.shape[0]
            copies.append(pltpu.make_async_copy(source, held.at[pl.ds(at, count)], sem.at[n]))
            at += count
    return copies


def project_kernel(rows, own, other, hop1, hop2, hop3, crossed, total, held, sem):
    copies = weight_loads((own, other, hop1, hop2, hop3, crossed), held, sem)
    start_all(copies)
    wait_all(copies)
    weight = held.reshape(14 * HD, 3 * HD)

    @pl.loop(0, 12)
    def _(n):
        here = pl.ds(pl.multiple_of(lax.rem(n, 4) * 128, 128), 128)
        there = pl.ds(pl.multiple_of(lax.div(n, 4) * HD, HD), HD)
        total[here, there] = jnp.dot(
            rows[here, : 14 * HD], weight[:, there], preferred_element_type=jnp.float32
        )


def attend_kernel(len_ref, rows, square, total, far, far_crossed, out, heads):
    @pl.loop(0, 2)
    def _(p):
        here = pl.ds(pl.multiple_of(p * PLEN, PLEN), PLEN)
        mean = jnp.sum(square[here, :], axis=1, keepdims=True) / D
        inverse = lax.rsqrt(mean + epsilon)

        @pl.loop(0, 3)
        def _(n):
            there = pl.ds(pl.multiple_of(n * HD, HD), HD)
            head = total[here, there]
            head += jnp.dot(rows[here, 14 * HD : 15 * HD], far[:, there], preferred_element_type=jnp.float32)
            head += jnp.dot(rows[here, 15 * HD :], far_crossed[:, there], preferred_element_type=jnp.float32)
            heads[n] = (head * inverse).astype(jnp.bfloat16)

        scores = lax.dot_general(
            heads[0], heads[1], (((1,), (1,)), ((), ())), preferred_element_type=jnp.float32
        ) * HD ** (-0.5)
        slot = lax.broadcasted_iota(jnp.int32, (PLEN, PLEN), 1)
        scores = jnp.where(slot < len_ref[p], scores, masked_score)
        expon = jnp.exp(scores - jnp.max(scores, axis=-1, keepdims=True))
        probs = (expon / jnp.sum(expon, axis=-1, keepdims=True)).astype(jnp.bfloat16)
        out[here, :] = jnp.dot(probs, heads[2], preferred_element_type=jnp.float32).astype(jnp.bfloat16)


def arrange_kernel(*refs):
    place = read(refs[0])
    parts, out, sem = refs[1:8], refs[8], refs[9]
    copies = []
    for n, (part, spot, row) in enumerate(late_places(place)):
        source = parts[part] if spot is None else parts[part].at[spot]
        copies.append(pltpu.make_async_copy(source, out.at[gather_spot(place, row)], sem.at[n]))
    start_all(copies)
    wait_all(copies)


def residual_near_kernel(*refs):
    parts, (weight, embedded, total) = refs[:6], refs[6:]

    @pl.loop(0, 4)
    def _(p):
        here = pl.ds(pl.multiple_of(p * 128, 128), 128)
        sum_here = embedded[here, :].astype(jnp.float32)
        for k in range(12):
            sum_here += jnp.dot(parts[k // 2][k % 2, here, :], weight[k], preferred_element_type=jnp.float32)
        total[here, :] = sum_here


def residual_far_kernel(far_back, far_ahead, weight, total, out, held, sem):
    load = pltpu.make_async_copy(weight.at[pl.ds(12, 4)], held, sem)
    load.start()
    load.wait()

    @pl.loop(0, 4)
    def _(p):
        here = pl.ds(pl.multiple_of(p * 128, 128), 128)
        sum_here = total[here, :]
        for k in range(SIDE):
            part = (far_back, far_ahead)[k // 2]
            sum_here += jnp.dot(part[k % 2, here, :], held[k], preferred_element_type=jnp.float32)
        out[here, :] = sum_here.astype(jnp.bfloat16)


def scaled(block, gain):
    wide = block.astype(jnp.float32)
    return (wide * gain).astype(jnp.bfloat16), lanes(wide * wide)


def cross_near_kernel(*refs):
    parts, (weight, gains, total, square) = refs[:6], refs[6:]

    @pl.loop(0, 4)
    def _(p):
        here = pl.ds(pl.multiple_of(p * 128, 128), 128)
        for k in range(12):
            block, squares = scaled(parts[k // 2][k % 2, here, :], gains[k])
            term = jnp.dot(block, weight[k], preferred_element_type=jnp.float32)
            total[here, :] = term if k == 0 else total[here, :] + term
            square[here, :] = squares if k == 0 else square[here, :] + squares


def cross_far_kernel(far_back, far_ahead, weight, gains, total, square, keys, values, held, sem):
    load = pltpu.make_async_copy(weight.at[pl.ds(12, 4)], held, sem)
    load.start()
    load.wait()

    @pl.loop(0, 4)
    def _(p):
        here = pl.ds(pl.multiple_of(p * 128, 128), 128)
        sum_here, squares = total[here, :], square[here, :]
        for k in range(SIDE):
            part = (far_back, far_ahead)[k // 2]
            block, more = scaled(part[k % 2, here, :], gains[12 + k])
            sum_here += jnp.dot(block, held[k], preferred_element_type=jnp.float32)
            squares += more
        inverse = lax.rsqrt(jnp.sum(squares, axis=1, keepdims=True) / D + epsilon)
        head = (sum_here * inverse).astype(jnp.bfloat16)
        keys[here, :] = head[:, :HD]
        values[here, :] = head[:, HD:]


def bf16(*shape):
    return jax.ShapeDtypeStruct(shape, jnp.bfloat16)


def f32(*shape):
    return jax.ShapeDtypeStruct(shape, jnp.float32)


def call(kernel, outs, ins, scratch, flops, moved, grant=28):
    return pl.pallas_call(
        kernel,
        out_shape=outs,
        in_specs=ins,
        out_specs=jax.tree.map(lambda _: VMEM, outs),
        scratch_shapes=scratch,
        compiler_params=pltpu.CompilerParams(vmem_limit_bytes=grant << 20),
        cost_estimate=pl.CostEstimate(flops=flops, bytes_accessed=moved, transcendentals=0),
    )


def pack_kernel(embedded, attn_gain, final_gain, out):
    tokens = embedded.shape[0]
    out[pl.ds(0, tokens), :] = embedded[...]
    place = lax.broadcasted_iota(jnp.int32, (GAIN_ROWS, HD), 0)
    first = jnp.broadcast_to(attn_gain[...].astype(jnp.float32).reshape(1, HD), (GAIN_ROWS, HD))
    second = jnp.broadcast_to(final_gain[...].astype(jnp.float32).reshape(1, HD), (GAIN_ROWS, HD))
    both = jnp.where(place == 0, first, jnp.where(place == 1, second, 0.0))
    out[pl.ds(tokens, GAIN_ROWS), :] = both.astype(jnp.bfloat16)


def join_kernel(*refs):
    parts, out, sem = refs[:-2], refs[-2], refs[-1]
    copies = [
        pltpu.make_async_copy(part, out.at[:, pl.ds(n * HD, HD)], sem.at[n]) for n, part in enumerate(parts)
    ]
    start_all(copies)
    wait_all(copies)


def side_by_side(*shards):
    return call(
        join_kernel,
        bf16(HD, len(shards) * HD),
        [HBM] * len(shards),
        [pltpu.SemaphoreType.DMA((len(shards),))],
        0,
        len(shards) << 17,
        grant=60,
    )(*shards)


def vmem(*shape, kind=jnp.bfloat16):
    return pltpu.VMEM(shape, kind)


def body(
    token_ids,
    passage_lengths,
    embedding,
    attn_gain,
    final_gain,
    query_weight,
    key_weight,
    value_weight,
    out_weight,
    crosskey_weight,
    crossvalue_weight,
):
    tokens = 2 * PLEN
    dma = pltpu.SemaphoreType.DMA((BLOCKS,))
    place = jnp.stack([lax.axis_index("row"), lax.axis_index("col")]).astype(jnp.int32)
    qkv_weight = side_by_side(query_weight, key_weight, value_weight)
    qkv_other = swap_cores(qkv_weight)
    early = gather_weight(qkv_weight, qkv_other, False)
    embedded = embedding.at[token_ids.reshape(-1)].get(mode="promise_in_bounds")
    chunk = call(
        pack_kernel, bf16(tokens + GAIN_ROWS, HD), [VMEM] * 3, [], 0, 1 << 19
    )(embedded, attn_gain, final_gain)
    parts = gather_direct(chunk)
    rows, square, gains = call(
        prepare_kernel,
        (bf16(tokens, D), f32(tokens, 128), f32(BLOCKS, 1, HD)),
        [SMEM] + [VMEM] * 4,
        [],
        100 * tokens * D * D // 16,
        8 << 20,
    )(place, *parts)
    total = call(
        project_kernel,
        f32(tokens, 3 * HD),
        [VMEM] + [ANY] * 6,
        [vmem(14, HD, 3 * HD), pltpu.SemaphoreType.DMA((6,))],
        2 * tokens * D * 3 * HD,
        10 << 20,
    )(rows, *early[:5], early[6])
    attended = call(
        attend_kernel,
        bf16(tokens, HD),
        [SMEM] + [VMEM] * 5,
        [vmem(3, PLEN, HD)],
        tokens * D * HD,
        4 << 20,
    )(passage_lengths, rows, square, total, early[5], early[7])
    late_weight = side_by_side(out_weight, crosskey_weight, crossvalue_weight)
    late_other = swap_cores(late_weight)
    outer = gather_weight(out_weight, late_other[:, :HD], True)
    cross = gather_weight(late_weight[:, HD:], late_other[:, HD:], True)

    def arrange(weight):
        width = weight[0].shape[1]
        return call(
            arrange_kernel, bf16(BLOCKS, HD, width), [SMEM] + [ANY] * 7, [dma], 0, 4 * D * width
        )(place, *weight)

    near, far = gather_split(attended)
    weight = arrange(outer)
    total = call(
        residual_near_kernel, f32(tokens, HD), [VMEM] * 8, [], 2 * tokens * D * HD, 6 << 20
    )(*near, weight, embedded)
    hidden = call(
        residual_far_kernel,
        bf16(tokens, HD),
        [VMEM, VMEM, ANY, VMEM],
        [vmem(SIDE, HD, HD), pltpu.SemaphoreType.DMA],
        tokens * D * HD // 2,
        2 << 20,
    )(*far, weight, total)
    near, far = gather_split(hidden)
    weight = arrange(cross)
    total, square = call(
        cross_near_kernel,
        (f32(tokens, 2 * HD), f32(tokens, 128)),
        [VMEM] * 8,
        [],
        4 * tokens * D * HD,
        8 << 20,
    )(*near, weight, gains)
    keys, values = call(
        cross_far_kernel,
        (bf16(tokens, HD), bf16(tokens, HD)),
        [VMEM, VMEM, ANY] + [VMEM] * 3,
        [vmem(SIDE, HD, 2 * HD), pltpu.SemaphoreType.DMA],
        tokens * D * HD,
        3 << 20,
    )(*far, weight, gains, total, square)
    return hidden, keys.reshape(tokens, 1, HD), values.reshape(tokens, 1, HD)


def solution(mesh):
    return jax.shard_map(
        body,
        mesh=mesh,
        in_specs=(
            P("row", None),
            P("row"),
            P(None, "col"),
            P("col"),
            P("col"),
            P("row", "col"),
            P("row", "col"),
            P("row", "col"),
            P("row", "col"),
            P("row", "col"),
            P("row", "col"),
        ),
        out_specs=(P("row", "col"), P("row", "col", None), P("row", "col", None)),
        check_vma=False,
    )
```

```python
import jax
import jax.numpy as jnp
from jax import lax
from jax.experimental import pallas as pl
from jax.experimental.pallas import tpu as pltpu
from jax.sharding import PartitionSpec as P

D = 4096
HD = 256
PLEN = 256
SIDE = 4
BLOCKS = SIDE * SIDE
GAIN_ROWS = 16

epsilon = 1e-06
masked_score = -1000000000.0


ANY = pl.BlockSpec(memory_space=pl.ANY)
SMEM = pl.BlockSpec(memory_space=pltpu.SMEM)
VMEM = pl.BlockSpec(memory_space=pltpu.VMEM)
HBM = pl.BlockSpec(memory_space=pltpu.HBM)

DEPTH = 8
SHIFTS = (1, 3, 2)
OFFSETS = (0, 3, 1, 2)


def moves(step):
    def index(z, c, x, y):
        return ((z % DEPTH * 2 + c) * SIDE + x % SIDE) * SIDE + y % SIDE

    return [
        (index(z, c, x, y), index(*step(z, c, x, y)))
        for z in range(DEPTH)
        for c in range(2)
        for x in range(SIDE)
        for y in range(SIDE)
    ]


def send(block, step):
    return lax.ppermute(block, ("row", "col"), moves(step))


def first_leg(block, shift):
    return send(block, lambda z, c, x, y: (z, c, x + shift * (1 - c), y + shift * c))


def second_leg(block, shift):
    return send(block, lambda z, c, x, y: (z, c, x + shift * c, y + shift * (1 - c)))


def along_z(block):
    return send(block, lambda z, c, x, y: (z + 1 - 2 * c, c, x, y))


def swap_cores(block):
    return send(block, lambda z, c, x, y: (z, 1 - c, x, y))


def gather_first(chunk):
    return jnp.stack([chunk] + [first_leg(chunk, s) for s in SHIFTS])


def gather_direct(chunk):
    stack = gather_first(chunk)
    return [stack] + [second_leg(stack, s) for s in SHIFTS]


def gather_split(chunk):
    back, ahead, far = (first_leg(chunk, s) for s in SHIFTS)
    low, high = jnp.stack([chunk, back]), jnp.stack([ahead, far])
    back_low, ahead_high = second_leg(low, 1), second_leg(high, 3)
    back_high, ahead_low = second_leg(high, 1), second_leg(low, 3)
    passed = [second_leg(back_low, 1), second_leg(ahead_high, 3)]
    return [low, high, back_low, back_high, ahead_low, ahead_high], passed


def gather_halved(chunk):
    stack = jnp.stack([chunk] + [first_leg(chunk, s) for s in SHIFTS])
    back, ahead = second_leg(stack, 1), second_leg(stack, 3)
    passed = [second_leg(back[:2], 1), second_leg(ahead[2:], 3)]
    return [stack, back, ahead], passed


def gather_weight(shard, other, late):
    block = jnp.stack([shard, other])
    parts = [shard, other]
    hops = []
    for hop in range(1, DEPTH // 2 + 1):
        block = along_z(block if hop < DEPTH // 2 else block[0])
        hops.append(block)
    if late:
        both = jnp.concatenate(hops[:3] + [hops[3][None]])
        return parts + hops + [swap_cores(both)]
    crossed = swap_cores(jnp.concatenate(hops[:3]))
    return parts + hops + [crossed, swap_cores(hops[3])]


def arrival(place, row):
    z, c = place[0], place[1]
    away = lax.rem((lax.div(row, 2) - z) * (1 - 2 * c) + DEPTH, DEPTH)
    same = jnp.where(lax.rem(row, 2) == c, 1, 0)
    near = jnp.where(away == 0, 1 - same, 14 + 1 - same)
    behind = 2 + 2 * (DEPTH - 1 - away) + 1 - same
    ahead = 8 + 2 * (away - 1) + same
    half = DEPTH // 2
    inner = jnp.where(away > half, behind, ahead)
    return jnp.where((away == 0) | (away == half), near, inner)


def late_places(place):
    z, c = place[0], place[1]
    up = 1 - 2 * c

    def row(depth, core):
        return lax.rem(depth + DEPTH, DEPTH) * 2 + core

    last = DEPTH // 2
    places = [(0, None, row(z, c)), (1, None, row(z, 1 - c))]
    for hop in range(1, last):
        places += [(1 + hop, 0, row(z - hop * up, c)), (1 + hop, 1, row(z - hop * up, 1 - c))]
        spot = 2 * hop - 2
        places += [(6, spot, row(z + hop * up, 1 - c)), (6, spot + 1, row(z + hop * up, c))]
    return places + [(5, None, row(z + last, c)), (6, 6, row(z + last, 1 - c))]


def gather_spot(place, row):
    c = place[1]
    away_x = lax.rem(lax.div(row, SIDE) - place[2] + SIDE, SIDE)
    away_y = lax.rem(lax.rem(row, SIDE) - place[3] + SIDE, SIDE)

    def index(away):
        return jnp.where(away == 0, 0, jnp.where(away == 3, 1, away + 1))

    first = index(away_x * (1 - c) + away_y * c)
    second = index(away_x * c + away_y * (1 - c))
    return second * SIDE + first


def block_of(place, first, second):
    c = place[1]
    x = place[2] + OFFSETS[first] * (1 - c) + OFFSETS[second] * c
    y = place[3] + OFFSETS[first] * c + OFFSETS[second] * (1 - c)
    return lax.rem(x, SIDE) * SIDE + lax.rem(y, SIDE)


def read(place_ref):
    row, col = place_ref[0], place_ref[1]
    return [lax.div(row, 2), lax.rem(row, 2), lax.div(col, SIDE), lax.rem(col, SIDE)]


def start_all(copies):
    for copy in copies:
        copy.start()


def wait_all(copies):
    for copy in copies:
        copy.wait()


def lanes(square):
    return sum(square[:, n * 128 : (n + 1) * 128] for n in range(square.shape[1] // 128))


def prepare_kernel(place_ref, own, back, ahead, far, rows, square, final_ref):
    place = read(place_ref)
    tokens, step = rows.shape[0], 64
    for second, part in enumerate((own, back, ahead, far)):
        for first in range(SIDE):
            spot = arrival(place, block_of(place, first, second))
            there = pl.ds(pl.multiple_of(spot * HD, HD), HD)
            gains = part[first, pl.ds(tokens, GAIN_ROWS), :].astype(jnp.float32)
            final_ref[second * SIDE + first] = gains[1:2, :]
            gain = gains[0:1, :]

            @pl.loop(0, tokens // step)
            def _(tile):
                here = pl.ds(pl.multiple_of(tile * step, step), step)
                wide = part[first, here, :].astype(jnp.float32)
                total = lanes(wide * wide)
                square[here, :] = total if second + first == 0 else square[here, :] + total
                rows[here, there] = (wide * gain).astype(jnp.bfloat16)


def weight_loads(sources, held, sem):
    copies, at = [], 0
    for n, source in enumerate(sources):
        if len(source.shape) == 2:
            copies.append(pltpu.make_async_copy(source, held.at[at], sem.at[n]))
            at += 1
        else:
            count = source.shape[0]
            copies.append(pltpu.make_async_copy(source, held.at[pl.ds(at, count)], sem.at[n]))
            at += count
    return copies


def project_kernel(rows, own, other, hop1, hop2, hop3, crossed, total, held, sem):
    copies = weight_loads((own, other, hop1, hop2, hop3, crossed), held, sem)
    start_all(copies)
    wait_all(copies)
    weight = held.reshape(14 * HD, 3 * HD)

    @pl.loop(0, 6)
    def _(n):
        here = pl.ds(pl.multiple_of(lax.div(n, 3) * PLEN, PLEN), PLEN)
        there = pl.ds(pl.multiple_of(lax.rem(n, 3) * HD, HD), HD)
        total[here, there] = jnp.dot(
            rows[here, : 14 * HD], weight[:, there], preferred_element_type=jnp.float32
        )


def attend_kernel(len_ref, rows, square, total, far, far_crossed, out, heads):
    @pl.loop(0, 2)
    def _(p):
        here = pl.ds(pl.multiple_of(p * PLEN, PLEN), PLEN)
        mean = jnp.sum(square[here, :], axis=1, keepdims=True) / D
        inverse = lax.rsqrt(mean + epsilon)
        for n in range(3):
            there = pl.ds(n * HD, HD)
            head = total[here, there]
            head += jnp.dot(rows[here, 14 * HD : 15 * HD], far[:, there], preferred_element_type=jnp.float32)
            head += jnp.dot(rows[here, 15 * HD :], far_crossed[:, there], preferred_element_type=jnp.float32)
            heads[n] = (head * inverse).astype(jnp.bfloat16)
        scores = lax.dot_general(
            heads[0], heads[1], (((1,), (1,)), ((), ())), preferred_element_type=jnp.float32
        ) * HD ** (-0.5)
        slot = lax.broadcasted_iota(jnp.int32, (PLEN, PLEN), 1)
        scores = jnp.where(slot < len_ref[p], scores, masked_score)
        expon = jnp.exp(scores - jnp.max(scores, axis=-1, keepdims=True))
        probs = (expon / jnp.sum(expon, axis=-1, keepdims=True)).astype(jnp.bfloat16)
        out[here, :] = jnp.dot(probs, heads[2], preferred_element_type=jnp.float32).astype(jnp.bfloat16)


def arrange_kernel(*refs):
    place = read(refs[0])
    parts, out, sem = refs[1:8], refs[8], refs[9]
    copies = []
    for n, (part, spot, row) in enumerate(late_places(place)):
        source = parts[part] if spot is None else parts[part].at[spot]
        copies.append(pltpu.make_async_copy(source, out.at[gather_spot(place, row)], sem.at[n]))
    start_all(copies)
    wait_all(copies)


def residual_near_kernel(*refs):
    parts, (weight, embedded, total) = refs[:6], refs[6:]

    @pl.loop(0, 4)
    def _(p):
        here = pl.ds(pl.multiple_of(p * 128, 128), 128)
        sum_here = embedded[here, :].astype(jnp.float32)
        for k in range(12):
            sum_here += jnp.dot(parts[k // 2][k % 2, here, :], weight[k], preferred_element_type=jnp.float32)
        total[here, :] = sum_here


def residual_far_kernel(far_back, far_ahead, weight, total, out, held, sem):
    load = pltpu.make_async_copy(weight.at[pl.ds(12, 4)], held, sem)
    load.start()
    load.wait()

    @pl.loop(0, 2)
    def _(p):
        here = pl.ds(pl.multiple_of(p * PLEN, PLEN), PLEN)
        sum_here = total[here, :]
        for k in range(SIDE):
            part = (far_back, far_ahead)[k // 2]
            sum_here += jnp.dot(part[k % 2, here, :], held[k], preferred_element_type=jnp.float32)
        out[here, :] = sum_here.astype(jnp.bfloat16)


def scaled(block, gain):
    wide = block.astype(jnp.float32)
    return (wide * gain).astype(jnp.bfloat16), lanes(wide * wide)


def cross_near_kernel(*refs):
    parts, (weight, gains, total, square) = refs[:3], refs[3:]

    @pl.loop(0, 4)
    def _(p):
        here = pl.ds(pl.multiple_of(p * 128, 128), 128)
        for k in range(12):
            block, squares = scaled(parts[k // SIDE][k % SIDE, here, :], gains[k])
            term = jnp.dot(block, weight[k], preferred_element_type=jnp.float32)
            total[here, :] = term if k == 0 else total[here, :] + term
            square[here, :] = squares if k == 0 else square[here, :] + squares


def cross_far_kernel(far_back, far_ahead, weight, gains, total, square, keys, values, held, sem):
    load = pltpu.make_async_copy(weight.at[pl.ds(12, 4)], held, sem)
    load.start()
    load.wait()

    @pl.loop(0, 4)
    def _(p):
        here = pl.ds(pl.multiple_of(p * 128, 128), 128)
        sum_here, squares = total[here, :], square[here, :]
        for k in range(SIDE):
            part = (far_back, far_ahead)[k // 2]
            block, more = scaled(part[k % 2, here, :], gains[12 + k])
            sum_here += jnp.dot(block, held[k], preferred_element_type=jnp.float32)
            squares += more
        inverse = lax.rsqrt(jnp.sum(squares, axis=1, keepdims=True) / D + epsilon)
        head = (sum_here * inverse).astype(jnp.bfloat16)
        keys[here, :] = head[:, :HD]
        values[here, :] = head[:, HD:]


def bf16(*shape):
    return jax.ShapeDtypeStruct(shape, jnp.bfloat16)


def f32(*shape):
    return jax.ShapeDtypeStruct(shape, jnp.float32)


def call(kernel, outs, ins, scratch, flops, moved, grant=28):
    return pl.pallas_call(
        kernel,
        out_shape=outs,
        in_specs=ins,
        out_specs=jax.tree.map(lambda _: VMEM, outs),
        scratch_shapes=scratch,
        compiler_params=pltpu.CompilerParams(vmem_limit_bytes=grant << 20),
        cost_estimate=pl.CostEstimate(flops=flops, bytes_accessed=moved, transcendentals=0),
    )


def pack_kernel(embedded, attn_gain, final_gain, out):
    tokens = embedded.shape[0]
    out[pl.ds(0, tokens), :] = embedded[...]
    place = lax.broadcasted_iota(jnp.int32, (GAIN_ROWS, HD), 0)
    first = jnp.broadcast_to(attn_gain[...].astype(jnp.float32).reshape(1, HD), (GAIN_ROWS, HD))
    second = jnp.broadcast_to(final_gain[...].astype(jnp.float32).reshape(1, HD), (GAIN_ROWS, HD))
    both = jnp.where(place == 0, first, jnp.where(place == 1, second, 0.0))
    out[pl.ds(tokens, GAIN_ROWS), :] = both.astype(jnp.bfloat16)


def join_kernel(*refs):
    parts, out, sem = refs[:-2], refs[-2], refs[-1]
    copies = [
        pltpu.make_async_copy(part, out.at[:, pl.ds(n * HD, HD)], sem.at[n]) for n, part in enumerate(parts)
    ]
    start_all(copies)
    wait_all(copies)


def side_by_side(*shards):
    return call(
        join_kernel,
        bf16(HD, len(shards) * HD),
        [HBM] * len(shards),
        [pltpu.SemaphoreType.DMA((len(shards),))],
        0,
        len(shards) << 17,
        grant=60,
    )(*shards)


def vmem(*shape, kind=jnp.bfloat16):
    return pltpu.VMEM(shape, kind)


def body(
    token_ids,
    passage_lengths,
    embedding,
    attn_gain,
    final_gain,
    query_weight,
    key_weight,
    value_weight,
    out_weight,
    crosskey_weight,
    crossvalue_weight,
):
    tokens = 2 * PLEN
    dma = pltpu.SemaphoreType.DMA((BLOCKS,))
    place = jnp.stack([lax.axis_index("row"), lax.axis_index("col")]).astype(jnp.int32)
    qkv_weight = side_by_side(query_weight, key_weight, value_weight)
    qkv_other = swap_cores(qkv_weight)
    early = gather_weight(qkv_weight, qkv_other, False)
    embedded = embedding.at[token_ids.reshape(-1)].get(mode="promise_in_bounds")
    chunk = call(
        pack_kernel, bf16(tokens + GAIN_ROWS, HD), [VMEM] * 3, [], 0, 1 << 19
    )(embedded, attn_gain, final_gain)
    parts = gather_direct(chunk)
    rows, square, gains = call(
        prepare_kernel,
        (bf16(tokens, D), f32(tokens, 128), f32(BLOCKS, 1, HD)),
        [SMEM] + [VMEM] * 4,
        [],
        100 * tokens * D * D // 16,
        8 << 20,
    )(place, *parts)
    total = call(
        project_kernel,
        f32(tokens, 3 * HD),
        [VMEM] + [ANY] * 6,
        [vmem(14, HD, 3 * HD), pltpu.SemaphoreType.DMA((6,))],
        2 * tokens * D * 3 * HD,
        10 << 20,
    )(rows, *early[:5], early[6])
    attended = call(
        attend_kernel,
        bf16(tokens, HD),
        [SMEM] + [VMEM] * 5,
        [vmem(3, PLEN, HD)],
        tokens * D * HD,
        4 << 20,
    )(passage_lengths, rows, square, total, early[5], early[7])
    late_weight = side_by_side(out_weight, crosskey_weight, crossvalue_weight)
    late_other = swap_cores(late_weight)
    outer = gather_weight(out_weight, late_other[:, :HD], True)
    cross = gather_weight(late_weight[:, HD:], late_other[:, HD:], True)

    def arrange(weight):
        width = weight[0].shape[1]
        return call(
            arrange_kernel,
            bf16(BLOCKS, HD, width),
            [SMEM] + [ANY] * 7,
            [dma],
            0,
            4 * D * width,
            grant=58,
        )(place, *weight)

    near, far = gather_split(attended)
    weight = arrange(outer)
    total = call(
        residual_near_kernel, f32(tokens, HD), [VMEM] * 8, [], 2 * tokens * D * HD, 6 << 20
    )(*near, weight, embedded)
    hidden = call(
        residual_far_kernel,
        bf16(tokens, HD),
        [VMEM, VMEM, ANY, VMEM],
        [vmem(SIDE, HD, HD), pltpu.SemaphoreType.DMA],
        tokens * D * HD // 2,
        2 << 20,
    )(*far, weight, total)
    near, far = gather_halved(hidden)
    weight = arrange(cross)
    total, square = call(
        cross_near_kernel,
        (f32(tokens, 2 * HD), f32(tokens, 128)),
        [VMEM] * 5,
        [],
        4 * tokens * D * HD,
        8 << 20,
    )(*near, weight, gains)
    keys, values = call(
        cross_far_kernel,
        (bf16(tokens, HD), bf16(tokens, HD)),
        [VMEM, VMEM, ANY] + [VMEM] * 3,
        [vmem(SIDE, HD, 2 * HD), pltpu.SemaphoreType.DMA],
        tokens * D * HD,
        3 << 20,
    )(*far, weight, gains, total, square)
    return hidden, keys.reshape(tokens, 1, HD), values.reshape(tokens, 1, HD)


def solution(mesh):
    return jax.shard_map(
        body,
        mesh=mesh,
        in_specs=(
            P("row", None),
            P("row"),
            P(None, "col"),
            P("col"),
            P("col"),
            P("row", "col"),
            P("row", "col"),
            P("row", "col"),
            P("row", "col"),
            P("row", "col"),
            P("row", "col"),
        ),
        out_specs=(P("row", "col"), P("row", "col", None), P("row", "col", None)),
        check_vma=False,
    )
```

```python
import jax
import jax.numpy as jnp
from jax import lax
from jax.experimental import pallas as pl
from jax.experimental.pallas import tpu as pltpu
from jax.sharding import PartitionSpec as P

D = 4096
HD = 256
PLEN = 256
SIDE = 4
BLOCKS = SIDE * SIDE
GAIN_ROWS = 16

epsilon = 1e-06
masked_score = -1000000000.0


ANY = pl.BlockSpec(memory_space=pl.ANY)
SMEM = pl.BlockSpec(memory_space=pltpu.SMEM)
VMEM = pl.BlockSpec(memory_space=pltpu.VMEM)
HBM = pl.BlockSpec(memory_space=pltpu.HBM)

DEPTH = 8
SHIFTS = (1, 3, 2)
OFFSETS = (0, 3, 1, 2)


def moves(step):
    def index(z, c, x, y):
        return ((z % DEPTH * 2 + c) * SIDE + x % SIDE) * SIDE + y % SIDE

    return [
        (index(z, c, x, y), index(*step(z, c, x, y)))
        for z in range(DEPTH)
        for c in range(2)
        for x in range(SIDE)
        for y in range(SIDE)
    ]


def send(block, step):
    return lax.ppermute(block, ("row", "col"), moves(step))


def first_leg(block, shift):
    return send(block, lambda z, c, x, y: (z, c, x + shift * (1 - c), y + shift * c))


def second_leg(block, shift):
    return send(block, lambda z, c, x, y: (z, c, x + shift * c, y + shift * (1 - c)))


def along_z(block):
    return send(block, lambda z, c, x, y: (z + 1 - 2 * c, c, x, y))


def swap_cores(block):
    return send(block, lambda z, c, x, y: (z, 1 - c, x, y))


def gather_first(chunk):
    return jnp.stack([chunk] + [first_leg(chunk, s) for s in SHIFTS])


def gather_direct(chunk):
    stack = gather_first(chunk)
    return [stack] + [second_leg(stack, s) for s in SHIFTS]


def gather_split(chunk):
    back, ahead, far = (first_leg(chunk, s) for s in SHIFTS)
    low, high = jnp.stack([chunk, back]), jnp.stack([ahead, far])
    back_low, ahead_high = second_leg(low, 1), second_leg(high, 3)
    back_high, ahead_low = second_leg(high, 1), second_leg(low, 3)
    passed = [second_leg(back_low, 1), second_leg(ahead_high, 3)]
    return [low, high, back_low, back_high, ahead_low, ahead_high], passed


def gather_weight(shard, other, late):
    block = jnp.stack([shard, other])
    parts = [shard, other]
    hops = []
    for hop in range(1, DEPTH // 2 + 1):
        block = along_z(block if hop < DEPTH // 2 else block[0])
        hops.append(block)
    if late:
        both = jnp.concatenate(hops[:3] + [hops[3][None]])
        return parts + hops + [swap_cores(both)]
    crossed = swap_cores(jnp.concatenate(hops[:3]))
    return parts + hops + [crossed, swap_cores(hops[3])]


def arrival(place, row):
    z, c = place[0], place[1]
    away = lax.rem((lax.div(row, 2) - z) * (1 - 2 * c) + DEPTH, DEPTH)
    same = jnp.where(lax.rem(row, 2) == c, 1, 0)
    near = jnp.where(away == 0, 1 - same, 14 + 1 - same)
    behind = 2 + 2 * (DEPTH - 1 - away) + 1 - same
    ahead = 8 + 2 * (away - 1) + same
    half = DEPTH // 2
    inner = jnp.where(away > half, behind, ahead)
    return jnp.where((away == 0) | (away == half), near, inner)


def late_places(place):
    z, c = place[0], place[1]
    up = 1 - 2 * c

    def row(depth, core):
        return lax.rem(depth + DEPTH, DEPTH) * 2 + core

    last = DEPTH // 2
    places = [(0, None, row(z, c)), (1, None, row(z, 1 - c))]
    for hop in range(1, last):
        places += [(1 + hop, 0, row(z - hop * up, c)), (1 + hop, 1, row(z - hop * up, 1 - c))]
        spot = 2 * hop - 2
        places += [(6, spot, row(z + hop * up, 1 - c)), (6, spot + 1, row(z + hop * up, c))]
    return places + [(5, None, row(z + last, c)), (6, 6, row(z + last, 1 - c))]


def gather_spot(place, row):
    c = place[1]
    away_x = lax.rem(lax.div(row, SIDE) - place[2] + SIDE, SIDE)
    away_y = lax.rem(lax.rem(row, SIDE) - place[3] + SIDE, SIDE)

    def index(away):
        return jnp.where(away == 0, 0, jnp.where(away == 3, 1, away + 1))

    first = index(away_x * (1 - c) + away_y * c)
    second = index(away_x * c + away_y * (1 - c))
    return second * SIDE + first


def block_of(place, first, second):
    c = place[1]
    away = jnp.where(first == 0, 0, jnp.where(first == 1, 3, first - 1))
    x = place[2] + away * (1 - c) + OFFSETS[second] * c
    y = place[3] + away * c + OFFSETS[second] * (1 - c)
    return lax.rem(x, SIDE) * SIDE + lax.rem(y, SIDE)


def read(place_ref):
    row, col = place_ref[0], place_ref[1]
    return [lax.div(row, 2), lax.rem(row, 2), lax.div(col, SIDE), lax.rem(col, SIDE)]


def start_all(copies):
    for copy in copies:
        copy.start()


def wait_all(copies):
    for copy in copies:
        copy.wait()


def lanes(square):
    return sum(square[:, n * 128 : (n + 1) * 128] for n in range(square.shape[1] // 128))


def prepare_kernel(place_ref, own, back, ahead, far, rows, square, final_ref):
    place = read(place_ref)
    tokens, step = rows.shape[0], 64
    square[...] = jnp.zeros_like(square)
    for second, part in enumerate((own, back, ahead, far)):

        @pl.loop(0, SIDE)
        def _(first):
            spot = arrival(place, block_of(place, first, second))
            there = pl.ds(pl.multiple_of(spot * HD, HD), HD)
            gains = part[first, pl.ds(tokens, GAIN_ROWS), :].astype(jnp.float32)
            final_ref[second * SIDE + first] = gains[1:2, :]
            gain = gains[0:1, :]

            @pl.loop(0, tokens // step)
            def _(tile):
                here = pl.ds(pl.multiple_of(tile * step, step), step)
                wide = part[first, here, :].astype(jnp.float32)
                square[here, :] += lanes(wide * wide)
                rows[here, there] = (wide * gain).astype(jnp.bfloat16)


def weight_loads(sources, held, sem):
    copies, at = [], 0
    for n, source in enumerate(sources):
        if len(source.shape) == 2:
            copies.append(pltpu.make_async_copy(source, held.at[at], sem.at[n]))
            at += 1
        else:
            count = source.shape[0]
            copies.append(pltpu.make_async_copy(source, held.at[pl.ds(at, count)], sem.at[n]))
            at += count
    return copies


def project_kernel(rows, own, other, hop1, hop2, hop3, crossed, total, held, sem):
    copies = weight_loads((own, other, hop1, hop2, hop3, crossed), held, sem)
    start_all(copies)
    wait_all(copies)
    weight = held.reshape(14 * HD, 3 * HD)

    @pl.loop(0, 6)
    def _(n):
        here = pl.ds(pl.multiple_of(lax.div(n, 3) * PLEN, PLEN), PLEN)
        there = pl.ds(pl.multiple_of(lax.rem(n, 3) * HD, HD), HD)
        total[here, there] = jnp.dot(
            rows[here, : 14 * HD], weight[:, there], preferred_element_type=jnp.float32
        )


def attend_kernel(len_ref, rows, square, total, far, far_crossed, out, heads):
    @pl.loop(0, 2)
    def _(p):
        here = pl.ds(pl.multiple_of(p * PLEN, PLEN), PLEN)
        mean = jnp.sum(square[here, :], axis=1, keepdims=True) / D
        inverse = lax.rsqrt(mean + epsilon)
        for n in range(3):
            there = pl.ds(n * HD, HD)
            head = total[here, there]
            head += jnp.dot(rows[here, 14 * HD : 15 * HD], far[:, there], preferred_element_type=jnp.float32)
            head += jnp.dot(rows[here, 15 * HD :], far_crossed[:, there], preferred_element_type=jnp.float32)
            heads[n] = (head * inverse).astype(jnp.bfloat16)
        scores = lax.dot_general(
            heads[0], heads[1], (((1,), (1,)), ((), ())), preferred_element_type=jnp.float32
        ) * HD ** (-0.5)
        slot = lax.broadcasted_iota(jnp.int32, (PLEN, PLEN), 1)
        scores = jnp.where(slot < len_ref[p], scores, masked_score)
        expon = jnp.exp(scores - jnp.max(scores, axis=-1, keepdims=True))
        probs = (expon / jnp.sum(expon, axis=-1, keepdims=True)).astype(jnp.bfloat16)
        out[here, :] = jnp.dot(probs, heads[2], preferred_element_type=jnp.float32).astype(jnp.bfloat16)


def arrange_kernel(*refs):
    place = read(refs[0])
    parts, out = refs[1:8], refs[8]
    for part, spot, row in late_places(place):
        source = parts[part] if spot is None else parts[part].at[spot]
        target = out.at[gather_spot(place, row)]

        @pl.loop(0, HD // 64)
        def _(tile):
            here = pl.ds(pl.multiple_of(tile * 64, 64), 64)
            target[here, :] = source[here, :]


def residual_near_kernel(*refs):
    parts, (weight, embedded, total) = refs[:6], refs[6:]

    @pl.loop(0, 4)
    def _(p):
        here = pl.ds(pl.multiple_of(p * 128, 128), 128)
        sum_here = embedded[here, :].astype(jnp.float32)
        for k in range(12):
            sum_here += jnp.dot(parts[k // 2][k % 2, here, :], weight[k], preferred_element_type=jnp.float32)
        total[here, :] = sum_here


def residual_far_kernel(far_back, far_ahead, weight, total, out, held, sem):
    load = pltpu.make_async_copy(weight.at[pl.ds(12, 4)], held, sem)
    load.start()
    load.wait()

    @pl.loop(0, 2)
    def _(p):
        here = pl.ds(pl.multiple_of(p * PLEN, PLEN), PLEN)
        sum_here = total[here, :]
        for k in range(SIDE):
            part = (far_back, far_ahead)[k // 2]
            sum_here += jnp.dot(part[k % 2, here, :], held[k], preferred_element_type=jnp.float32)
        out[here, :] = sum_here.astype(jnp.bfloat16)


def scaled(block, gain):
    wide = block.astype(jnp.float32)
    return (wide * gain).astype(jnp.bfloat16), lanes(wide * wide)


def cross_near_kernel(*refs):
    parts, (weight, gains, total, square) = refs[:6], refs[6:]

    @pl.loop(0, 4)
    def _(p):
        here = pl.ds(pl.multiple_of(p * 128, 128), 128)
        for k in range(12):
            block, squares = scaled(parts[k // 2][k % 2, here, :], gains[k])
            term = jnp.dot(block, weight[k], preferred_element_type=jnp.float32)
            total[here, :] = term if k == 0 else total[here, :] + term
            square[here, :] = squares if k == 0 else square[here, :] + squares


def cross_far_kernel(far_back, far_ahead, weight, gains, total, square, keys, values, held, sem):
    load = pltpu.make_async_copy(weight.at[pl.ds(12, 4)], held, sem)
    load.start()
    load.wait()

    @pl.loop(0, 4)
    def _(p):
        here = pl.ds(pl.multiple_of(p * 128, 128), 128)
        sum_here, squares = total[here, :], square[here, :]
        for k in range(SIDE):
            part = (far_back, far_ahead)[k // 2]
            block, more = scaled(part[k % 2, here, :], gains[12 + k])
            sum_here += jnp.dot(block, held[k], preferred_element_type=jnp.float32)
            squares += more
        inverse = lax.rsqrt(jnp.sum(squares, axis=1, keepdims=True) / D + epsilon)
        head = (sum_here * inverse).astype(jnp.bfloat16)
        keys[here, :] = head[:, :HD]
        values[here, :] = head[:, HD:]


def bf16(*shape):
    return jax.ShapeDtypeStruct(shape, jnp.bfloat16)


def f32(*shape):
    return jax.ShapeDtypeStruct(shape, jnp.float32)


def call(kernel, outs, ins, scratch, flops, moved, grant=16):
    return pl.pallas_call(
        kernel,
        out_shape=outs,
        in_specs=ins,
        out_specs=jax.tree.map(lambda _: VMEM, outs),
        scratch_shapes=scratch,
        compiler_params=pltpu.CompilerParams(vmem_limit_bytes=grant << 20),
        cost_estimate=pl.CostEstimate(flops=flops, bytes_accessed=moved, transcendentals=0),
    )


def pack_kernel(embedded, attn_gain, final_gain, out):
    tokens = embedded.shape[0]
    out[pl.ds(0, tokens), :] = embedded[...]
    place = lax.broadcasted_iota(jnp.int32, (GAIN_ROWS, HD), 0)
    first = jnp.broadcast_to(attn_gain[...].astype(jnp.float32).reshape(1, HD), (GAIN_ROWS, HD))
    second = jnp.broadcast_to(final_gain[...].astype(jnp.float32).reshape(1, HD), (GAIN_ROWS, HD))
    both = jnp.where(place == 0, first, jnp.where(place == 1, second, 0.0))
    out[pl.ds(tokens, GAIN_ROWS), :] = both.astype(jnp.bfloat16)


def join_kernel(*refs):
    parts, out, sem = refs[:-2], refs[-2], refs[-1]
    copies = [
        pltpu.make_async_copy(part, out.at[:, pl.ds(n * HD, HD)], sem.at[n]) for n, part in enumerate(parts)
    ]
    start_all(copies)
    wait_all(copies)


def side_by_side(*shards):
    return call(
        join_kernel,
        bf16(HD, len(shards) * HD),
        [HBM] * len(shards),
        [pltpu.SemaphoreType.DMA((len(shards),))],
        0,
        len(shards) << 17,
        grant=60,
    )(*shards)


def vmem(*shape, kind=jnp.bfloat16):
    return pltpu.VMEM(shape, kind)


def body(
    token_ids,
    passage_lengths,
    embedding,
    attn_gain,
    final_gain,
    query_weight,
    key_weight,
    value_weight,
    out_weight,
    crosskey_weight,
    crossvalue_weight,
):
    tokens = 2 * PLEN
    place = jnp.stack([lax.axis_index("row"), lax.axis_index("col")]).astype(jnp.int32)
    qkv_weight = side_by_side(query_weight, key_weight, value_weight)
    qkv_other = swap_cores(qkv_weight)
    early = gather_weight(qkv_weight, qkv_other, False)
    embedded = embedding.at[token_ids.reshape(-1)].get(mode="promise_in_bounds")
    chunk = call(
        pack_kernel, bf16(tokens + GAIN_ROWS, HD), [VMEM] * 3, [], 0, 1 << 19
    )(embedded, attn_gain, final_gain)
    parts = gather_direct(chunk)
    rows, square, gains = call(
        prepare_kernel,
        (bf16(tokens, D), f32(tokens, 128), f32(BLOCKS, 1, HD)),
        [SMEM] + [VMEM] * 4,
        [],
        100 * tokens * D * D // 16,
        8 << 20,
    )(place, *parts)
    total = call(
        project_kernel,
        f32(tokens, 3 * HD),
        [VMEM] + [ANY] * 6,
        [vmem(14, HD, 3 * HD), pltpu.SemaphoreType.DMA((6,))],
        2 * tokens * D * 3 * HD,
        10 << 20,
    )(rows, *early[:5], early[6])
    attended = call(
        attend_kernel,
        bf16(tokens, HD),
        [SMEM] + [VMEM] * 5,
        [vmem(3, PLEN, HD)],
        tokens * D * HD,
        4 << 20,
    )(passage_lengths, rows, square, total, early[5], early[7])
    late_weight = side_by_side(out_weight, crosskey_weight, crossvalue_weight)
    late_other = swap_cores(late_weight)
    outer = gather_weight(out_weight, late_other[:, :HD], True)
    cross = gather_weight(late_weight[:, HD:], late_other[:, HD:], True)

    def arrange(weight):
        width = weight[0].shape[1]
        return call(
            arrange_kernel, bf16(BLOCKS, HD, width), [SMEM] + [VMEM] * 7, [], 0, 4 * D * width
        )(place, *weight)

    near, far = gather_split(attended)
    weight = arrange(outer)
    total = call(
        residual_near_kernel, f32(tokens, HD), [VMEM] * 8, [], 2 * tokens * D * HD, 6 << 20
    )(*near, weight, embedded)
    hidden = call(
        residual_far_kernel,
        bf16(tokens, HD),
        [VMEM, VMEM, ANY, VMEM],
        [vmem(SIDE, HD, HD), pltpu.SemaphoreType.DMA],
        tokens * D * HD // 2,
        2 << 20,
    )(*far, weight, total)
    near, far = gather_split(hidden)
    weight = arrange(cross)
    total, square = call(
        cross_near_kernel,
        (f32(tokens, 2 * HD), f32(tokens, 128)),
        [VMEM] * 8,
        [],
        4 * tokens * D * HD,
        8 << 20,
    )(*near, weight, gains)
    keys, values = call(
        cross_far_kernel,
        (bf16(tokens, HD), bf16(tokens, HD)),
        [VMEM, VMEM, ANY] + [VMEM] * 3,
        [vmem(SIDE, HD, 2 * HD), pltpu.SemaphoreType.DMA],
        tokens * D * HD,
        3 << 20,
    )(*far, weight, gains, total, square)
    return hidden, keys.reshape(tokens, 1, HD), values.reshape(tokens, 1, HD)


def solution(mesh):
    return jax.shard_map(
        body,
        mesh=mesh,
        in_specs=(
            P("row", None),
            P("row"),
            P(None, "col"),
            P("col"),
            P("col"),
            P("row", "col"),
            P("row", "col"),
            P("row", "col"),
            P("row", "col"),
            P("row", "col"),
            P("row", "col"),
        ),
        out_specs=(P("row", "col"), P("row", "col", None), P("row", "col", None)),
        check_vma=False,
    )
```
